32 devices in a mesh: tok: 2 (over y), lat: 16 (over z, x, core).
Axes of the slice: x: 2, y: 2, z: 4, core: 2. Of those that a mesh axis runs over, the one named last changes fastest.
Arguments:
- tokens: bfloat16 [512, 8192], P(('tok', 'lat')), may hold values from -6 to 6
- enc_weight: bfloat16 [8192, 4096], P(None, 'lat'), may hold values from -0.0625 to 0.0625
- enc_bias: float32 [4096], P('lat'), may hold values from -3 to 3
- dec_weight: bfloat16 [4096, 8192], P('lat'), may hold values from -0.125 to 0.125
- dec_bias: float32 [8192], replicated, may hold values from -3 to 3
- active_blocks: int32 [4, 8], P('tok'), may hold values from 0 to 15, all different within a row
Outputs:
- reconstruction: bfloat16 [512, 8192], P(('tok', 'lat'))
- enc_grad: float32 [8192, 4096], P('tok', 'lat')
- dec_grad: float32 [4096, 8192], P('lat', 'tok')
The draws below stay inside these ranges and needn't reach their ends.
Inputs may be any that keep to these rules, and one draw needn't show every extreme that they name: `active_blocks`: each row lists 8 different latent blocks, and every latent block is listed by some row.
All inputs are finite; a program needn't handle non-finite values.
Results may differ from the reference program's by a relative error of at most 0.013.
Values may be sent and summed in bfloat16 or wider, within the bound.
A program may use at most 64 MiB of HBM per device.

```python
import math
import jax
import jax.numpy as jnp
from jax import lax

D = 8192
LB = 256
BLK = 128
BLK_DEV = 1
SLOTS = 8
GB = 2
NB = 16
LATENTS = 4096
TOKEN_BLOCKS = 4
TOKENS = 512
GROUP = 256
N_LAT = 16


def block_scale(stream_key, extent, cuts, least, top_value):
    def one(axis_at, blocks):
        steps = jax.random.uniform(jax.random.fold_in(jax.random.fold_in(stream_key, 6), axis_at), (blocks,), jnp.float32, least / len(cuts), top_value / len(cuts))
        return jnp.repeat(jnp.exp(steps), extent[axis_at] // blocks).reshape((-1,) + (1,) * (len(extent) - axis_at - 1))

    level = one(*cuts[0])
    for cut in cuts[1:]:
        level = level * one(*cut)
    return level


def choose_distinct(stream_key, rows, count, top, lift):
    order = jax.random.permutation(jax.random.fold_in(stream_key, 1), count)
    pull = order
    for power in range(3):
        pull = pull * pull // count
    pull = pull * lift // count
    tickets = jax.random.randint(jax.random.fold_in(stream_key, 2), (rows, count), 0, 4096) + pull
    fixed_rows = jax.random.permutation(jax.random.fold_in(stream_key, 3), rows)[jnp.arange(count) % rows]
    tickets = jnp.where(jnp.arange(rows)[:, None] == fixed_rows[None, :], 1 << 14, tickets)
    priority = tickets * count + jnp.arange(count)
    return lax.top_k(priority.astype(jnp.int32), top)[1].astype(jnp.int32)


def noise(key, shape, scale, limit, cuts=(), kind=jnp.bfloat16):
    gain = block_scale(key, shape, cuts, -0.22, 0.18) if cuts else 1.0
    entries = jax.random.normal(key, shape, jnp.float32) * scale * gain
    return jnp.minimum(jnp.maximum(entries, -limit), limit).astype(kind)


def setup_inputs(seed: int = 0) -> dict:
    streams_of = jax.random.split(jax.random.key(seed), 7)
    tokens = noise(streams_of[0], (TOKENS, D), 1.0, 6.0, ((0, 32),))
    enc_weight = noise(streams_of[1], (D, LATENTS), D ** -0.5, 0.0625, ((1, 16),))
    enc_bias = noise(streams_of[2], (LATENTS,), 0.5, 3.0, ((0, 16),), jnp.float32)
    dec_weight = noise(streams_of[3], (LATENTS, D), (SLOTS * LB) ** -0.5, 0.125, ((0, 16),))
    dec_bias = noise(streams_of[4], (D,), 0.5, 3.0, (), jnp.float32)
    active_blocks = choose_distinct(streams_of[5], TOKEN_BLOCKS, NB, SLOTS, 8192)
    return dict(tokens=tokens, enc_weight=enc_weight, enc_bias=enc_bias, dec_weight=dec_weight, dec_bias=dec_bias, active_blocks=active_blocks)


def reference(tokens, enc_weight, enc_bias, dec_weight, dec_bias, active_blocks):
    latent_width = BLK_DEV * LB
    block_ids = jnp.arange(NB, dtype=jnp.int32)
    block_hits = jnp.any(active_blocks[:, :, None] == block_ids[None, None, :], axis=1).astype(jnp.float32)
    latent_gate = jnp.repeat(jnp.repeat(block_hits, LB, axis=1), BLK, axis=0)
    pre_act = jnp.dot(tokens, enc_weight, preferred_element_type=jnp.float32) + enc_bias.astype(jnp.float32)[None, :]
    activations = (jax.nn.silu(pre_act) * latent_gate).astype(jnp.bfloat16)

    def owner_term(running, owner_index):
        first_col = (owner_index * latent_width).astype(jnp.int32)
        owner_acts = lax.dynamic_slice_in_dim(activations, first_col, latent_width, 1)
        owner_rows = lax.dynamic_slice_in_dim(dec_weight, first_col, latent_width, 0)
        owner_part = jnp.dot(owner_acts, owner_rows, preferred_element_type=jnp.float32)
        owner_part = lax.optimization_barrier(owner_part.astype(jnp.bfloat16))
        return (running + owner_part.astype(jnp.float32), None)
    summed, _ = lax.scan(owner_term, jnp.zeros((TOKENS, D), jnp.float32), jnp.arange(N_LAT, dtype=jnp.int32))
    decoded = summed + dec_bias.astype(jnp.float32)[None, :]
    reconstruction = decoded.astype(jnp.bfloat16)
    cotangent = ((decoded - tokens.astype(jnp.float32)) * (1.0 / math.sqrt(TOKENS))).astype(jnp.bfloat16)
    latent_grad = jnp.dot(cotangent, dec_weight.T, preferred_element_type=jnp.float32)
    sigma = jax.nn.sigmoid(pre_act)
    pre_grad = (latent_grad * (sigma * (1.0 + pre_act * (1.0 - sigma))) * latent_gate).astype(jnp.bfloat16)

    def group_term(totals, group_index):
        enc_total, dec_total = totals
        first_row = (group_index * GROUP).astype(jnp.int32)
        group_tokens = lax.dynamic_slice_in_dim(tokens, first_row, GROUP, 0)
        group_grad = lax.dynamic_slice_in_dim(pre_grad, first_row, GROUP, 0)
        group_acts = lax.dynamic_slice_in_dim(activations, first_row, GROUP, 0)
        group_cot = lax.dynamic_slice_in_dim(cotangent, first_row, GROUP, 0)
        enc_part = jnp.dot(group_tokens.T, group_grad, preferred_element_type=jnp.float32)
        enc_part = lax.optimization_barrier(enc_part.astype(jnp.bfloat16))
        dec_part = jnp.dot(group_acts.T, group_cot, preferred_element_type=jnp.float32)
        dec_part = lax.optimization_barrier(dec_part.astype(jnp.bfloat16))
        return ((enc_total + enc_part.astype(jnp.float32), dec_total + dec_part.astype(jnp.float32)), None)
    start_totals = (jnp.zeros((D, LATENTS), jnp.float32), jnp.zeros((LATENTS, D), jnp.float32))
    totals, _ = lax.scan(group_term, start_totals, jnp.arange(TOKEN_BLOCKS // GB, dtype=jnp.int32))
    return (reconstruction, totals[0], totals[1])
```

```python
import functools
import math

import jax
import jax.numpy as jnp
from jax import lax
from jax.experimental import pallas as pl
from jax.experimental.pallas import tpu as pltpu
from jax.sharding import PartitionSpec as P

LB = 256
MESH = pl.DeviceIdType.MESH
NZ, NX, NC = 4, 2, 2
BF16 = jnp.bfloat16
F32 = jnp.float32


def contract_rows(left_rows, right_rows):
    return lax.dot_general(
        left_rows, right_rows, (((0,), (0,)), ((), ())), preferred_element_type=jnp.float32
    )


def fused_kernel(
    cot_scale,
    tok_hbm, encw_hbm, encb_ref, decw_hbm, decb_ref, blocks_ref,
    recon_ref, encg_ref, decg_ref,
    encw, decw, decw_o, TY, RY, X, XT, D, C, P, RX, RX0, RP, RI,
    pre, pre_s, pre_o, act, act_o, act_t, lg, lg_s, lg_o, pg, gate, eg, dg,
    local_sem, out_sem, send_sem, y_recv, tok_recv, tokc_recv, dec_recv, decc_recv,
    rx_recv, rx0_recv, rp_recv, ri_recv, small_recv,
):
    t = lax.axis_index("tok")
    l = lax.axis_index("lat")
    z, x, c = l // (NX * NC), (l // NC) % NX, l % NC
    rows, width = tok_hbm.shape
    half = width // 2
    quarter = half // 2
    locs = NZ * NX
    chunk_rows = 2 * locs * rows
    latents = encw.shape[1]

    def loc(zz, xx):
        return zz * NX + xx

    ox, ot = 1 - x, 1 - t
    here = loc(z, x)
    pair_z = z + 1 - 2 * lax.rem(z, 2)
    near = z // 2
    sources = (pair_z, 2 - near, 3 - 3 * near)
    line_same = [here] + [loc(zz, x) for zz in sources]
    line_other = [loc(z, ox)] + [loc(zz, ox) for zz in sources]
    near_loc = [[loc(2 * near + j, x), loc(2 * near + j, ox)] for j in range(2)]
    far_loc = [[loc(2 - 2 * near + j, x), loc(2 - 2 * near + j, ox)] for j in range(2)]
    col = [x, ox]
    inside = jnp.logical_and(z >= 1, z <= 2)
    outside = jnp.logical_not(inside)
    pair = (t, loc(pair_z, x) * NC + c)
    inner = (t, loc(3 - z, x) * NC + c)
    x_peer = (t, loc(z, ox) * NC + c)
    c_peer = (t, here * NC + 1 - c)
    y_peer = (ot, l)

    mine = pl.ds(pl.multiple_of(t * half, half), half)
    theirs = pl.ds(pl.multiple_of(ot * half, half), half)
    qc = pl.ds(pl.multiple_of(c * quarter, quarter), quarter)
    qo = pl.ds(pl.multiple_of((1 - c) * quarter, quarter), quarter)
    sent_q = pl.ds(pl.multiple_of(t * half + (1 - c) * quarter, quarter), quarter)

    local = [
        pltpu.make_async_copy(tok_hbm.at[:, mine], X.at[c, t, here], local_sem.at[0]),
        pltpu.make_async_copy(tok_hbm.at[:, theirs], TY, local_sem.at[1]),
        pltpu.make_async_copy(encw_hbm.at[mine], encw, local_sem.at[2]),
        pltpu.make_async_copy(decw_hbm.at[:, mine], decw, local_sem.at[3]),
    ]
    for copy in local:
        copy.start()

    block_count = blocks_ref.shape[0]
    for b in range(block_count):
        hit = blocks_ref[b, 0] == l
        for slot in range(1, blocks_ref.shape[1]):
            hit = jnp.logical_or(hit, blocks_ref[b, slot] == l)
        gate[t, b] = jnp.broadcast_to(jnp.where(hit, 1.0, 0.0).astype(F32), gate.shape[2:])

    barrier = pltpu.get_barrier_semaphore()
    peers = [pair, inner, x_peer, c_peer, y_peer]
    for peer in peers:
        pl.semaphore_signal(barrier, inc=1, device_id=peer, device_id_type=MESH)
    pl.semaphore_wait(barrier, len(peers))

    shape_of = {
        "q": P.at[0, 0, 0], "f": TY, "s": act.at[0], "d": decw_o, "g": gate.at[0],
    }
    sends = {"all": [], "inside": [], "outside": [], "c0": [], "c1": []}
    flags = {"inside": inside, "outside": outside, "c0": c == 0, "c1": c == 1}
    count = [0]

    def push(kind, src, dst, recv, peer, who="all"):
        sem = count[0]
        count[0] += 1
        pltpu.make_async_remote_copy(
            src_ref=src, dst_ref=dst, send_sem=send_sem.at[sem], recv_sem=recv,
            device_id=peer, device_id_type=MESH,
        ).start()
        sends[who].append((kind, sem))

    def arrived(dst, recv):
        pltpu.make_async_remote_copy(
            src_ref=dst, dst_ref=dst, send_sem=send_sem.at[0], recv_sem=recv,
            device_id=c_peer, device_id_type=MESH,
        ).wait_recv()

    def finish_sends():
        for who, items in sends.items():
            def go(items=items):
                for kind, sem in items:
                    ref = shape_of[kind]
                    pltpu.make_async_remote_copy(
                        src_ref=ref, dst_ref=ref, send_sem=send_sem.at[sem],
                        recv_sem=small_recv.at[0], device_id=c_peer, device_id_type=MESH,
                    ).wait_send()
            if who == "all":
                go()
            elif items:
                pl.when(flags[who])(go)
            sends[who] = []

    def group_of(k):
        return t if k == 0 else ot

    def tok_ref(p, s):
        cc, k = p
        tt = group_of(k)
        return X.at[cc, tt, s, :, qc], tok_recv.at[(cc * 2 + tt) * locs + s]

    def tok_give(p, s, peer, who="all"):
        ref, sem = tok_ref(p, s)
        push("q", ref, ref, sem, peer, who)

    def tok_give_c(p, s):
        cc, k = p
        ref, _ = tok_ref(p, s)
        push("q", ref, ref, tokc_recv.at[(cc * 2 + group_of(k)) * locs + s], c_peer)

    def tok_own(p):
        cc, k = p
        tt = group_of(k)
        whole = X.at[cc, tt, here]
        csem = tokc_recv.at[(cc * 2 + tt) * locs + here]

        @pl.when(c == cc)
        def _():
            if k == 0:
                local[0].wait()
            else:
                arrived(whole, y_recv.at[0])
            push("f", whole, whole, csem, c_peer, f"c{cc}")

        @pl.when(c != cc)
        def _():
            arrived(whole, csem)

        tok_give(p, here, pair)
        tok_give(p, here, x_peer)
        pl.when(inside)(lambda: tok_give(p, here, inner, "inside"))

    def tok_z(p, i):
        s = line_same[1 + i]
        ref, sem = tok_ref(p, s)
        arrived(ref, sem)
        pl.when(inside)(lambda: tok_give(p, s, inner if i == 0 else pair, "inside"))
        tok_give(p, s, x_peer)
        tok_give_c(p, s)

    def tok_x(p, i):
        s = line_other[i]
        ref, sem = tok_ref(p, s)
        arrived(ref, sem)
        tok_give_c(p, s)

    def tok_settle(cc):
        for tt in range(2):
            for s in line_same[1:] + line_other:
                arrived(X.at[cc, tt, s, :, qo], tokc_recv.at[(cc * 2 + tt) * locs + s])

    part = [pl.ds(cc * chunk_rows, chunk_rows) for cc in range(2)]
    tile = 1024

    def encode(cc):
        pre[cc] = jnp.dot(
            X[cc, :, :, :, :tile].reshape(chunk_rows, tile), encw[:tile, :],
            preferred_element_type=F32,
        )

        @pl.loop(1, half // tile)
        def _(k):
            cols = pl.ds(pl.multiple_of(k * tile, tile), tile)
            pre[cc] += jnp.dot(
                X[cc, :, :, :, cols].reshape(chunk_rows, tile), encw[cols, :],
                preferred_element_type=F32,
            )
        pre_s[cc] = pre[cc].astype(BF16)
        push("s", pre_s.at[cc], pre_o.at[cc], small_recv.at[cc], y_peer)

    tile_t = 512

    def transpose_tokens(cc):
        @pl.loop(0, half // tile_t)
        def _(k):
            cols = pl.ds(pl.multiple_of(k * tile_t, tile_t), tile_t)
            XT[cols, part[cc]] = X[cc, :, :, :, cols].reshape(chunk_rows, tile_t).T

    seg_rows = locs * rows // block_count

    def segments():
        for tt in range(2):
            for b in range(block_count):
                at = (tt * block_count + b) * seg_rows
                yield slice(at, at + seg_rows), gate[tt, b][:1, :]

    def activate(cc):
        arrived(pre_o.at[cc], small_recv.at[cc])
        for seg, g in segments():
            v = pre[cc, seg, :] + pre_o[cc, seg, :].astype(F32) + encb_ref[...]
            pre[cc, seg, :] = v
            act[cc, seg, :] = (v * jax.nn.sigmoid(v) * g).astype(BF16)
        push("s", act.at[cc], act_o.at[cc], small_recv.at[2 + cc], c_peer)

    def slopes(cc):
        act_t[:, part[cc]] = act[cc].T
        for seg, g in segments():
            v = pre[cc, seg, :]
            sigma = jax.nn.sigmoid(v)
            pre[cc, seg, :] = sigma * (1.0 + v * (1.0 - sigma)) * g

    tile_d = 512

    def decode(cc):
        arrived(act_o.at[cc], small_recv.at[2 + cc])

        @pl.loop(0, quarter // tile_d)
        def _(k):
            cols = pl.ds(pl.multiple_of(k * tile_d, tile_d), tile_d)
            own_cols = pl.ds(pl.multiple_of(c * quarter + k * tile_d, tile_d), tile_d)
            term = jnp.dot(act[cc], decw[:, own_cols], preferred_element_type=F32)
            term = term + jnp.dot(act_o[cc], decw_o[:, cols], preferred_element_type=F32)
            P[cc, :, :, :, cols] = term.astype(BF16).reshape(2, locs, rows, tile_d)

    def term(cc, tt, s):
        return P.at[cc, tt, s]

    def add(dst, *terms):
        total = dst[...].astype(F32)
        for other in terms:
            total = total + other[...].astype(F32)
        dst[...] = total.astype(BF16)

    def rp(cc, slot):
        return RP.at[cc, slot], rp_recv.at[cc * 6 + slot]

    def ri(cc, slot):
        return RI.at[cc, slot], ri_recv.at[cc * 6 + slot]

    def rx(cc, slot):
        return RX.at[cc, slot], rx_recv.at[cc * 4 + slot]

    def rx0(cc, slot):
        return RX0.at[cc, slot], rx0_recv.at[cc * 2 + slot]

    both = [(j, d) for d in (1, 0) for j in range(2)]

    def sum_start(cc):
        for j in range(2):
            dst, sem = rx(cc, j)
            push("q", term(cc, 1, far_loc[j][1]), dst, sem, x_peer)

        @pl.when(outside)
        def _():
            for j, d in both:
                dst, sem = rp(cc, j * 2 + col[d])
                push("q", term(cc, 0, far_loc[j][d]), dst, sem, pair, "outside")
        for j in range(2):
            dst, sem = rx(cc, 2 + j)
            push("q", term(cc, 1, near_loc[j][1]), dst, sem, x_peer)

    def sum_far(cc):
        for j in range(2):
            src, sem = rx(cc, j)
            arrived(src, sem)

        @pl.when(outside)
        def _():
            for j in range(2):
                src, _ = rx(cc, j)
                dst, sem = rp(cc, 4 + j)
                mid = term(cc, 1, far_loc[j][0])
                add(mid, src)
                push("q", mid, dst, sem, pair, "outside")

        @pl.when(inside)
        def _():
            for j, d in both:
                src, sem = rp(cc, j * 2 + col[d])
                arrived(src, sem)
                mid = term(cc, 0, far_loc[j][d])
                add(mid, src)
                dst, sem = ri(cc, j * 2 + col[d])
                push("q", mid, dst, sem, inner, "inside")
            for j in range(2):
                src, sem = rp(cc, 4 + j)
                arrived(src, sem)
                mid = term(cc, 1, far_loc[j][0])
                add(mid, src, rx(cc, j)[0])
                dst, sem = ri(cc, 4 + j)
                push("q", mid, dst, sem, inner, "inside")
        for j in range(2):
            src, sem = rx(cc, 2 + j)
            arrived(src, sem)
            add(term(cc, 1, near_loc[j][0]), src)

    def sum_near(cc):
        @pl.when(inside)
        def _():
            for j, d in both:
                src, sem = ri(cc, j * 2 + col[d])
                arrived(src, sem)
                mid = term(cc, 0, near_loc[j][d])
                add(mid, src)
                dst, sem = rp(cc, j * 2 + col[d])
                push("q", mid, dst, sem, pair, "inside")
            for j in range(2):
                src, sem = ri(cc, 4 + j)
                arrived(src, sem)
                mid = term(cc, 1, near_loc[j][0])
                add(mid, src)
                dst, sem = rp(cc, 4 + j)
                push("q", mid, dst, sem, pair, "inside")

    def dec_ref(cc, tt, s):
        return D.at[cc, tt, s, :, qc], dec_recv.at[(cc * 2 + tt) * locs + s]

    def dec_give(cc, tt, s, peer, who="all"):
        ref, sem = dec_ref(cc, tt, s)
        push("q", ref, ref, sem, peer, who)

    def dec_give_c(cc, tt, s, who="all"):
        ref, _ = dec_ref(cc, tt, s)
        push("q", ref, ref, decc_recv.at[(cc * 2 + tt) * locs + s], c_peer, who)

    def dec_take(cc, tt, s):
        arrived(*dec_ref(cc, tt, s))

    bias_cols = pl.ds(pl.multiple_of(t * half + c * quarter, quarter), quarter)

    def sum_last(cc):
        @pl.when(outside)
        def _():
            for j, d in both:
                src, sem = rp(cc, j * 2 + col[d])
                arrived(src, sem)
                mid = term(cc, 0, near_loc[j][d])
                add(mid, src)
                if d == 1:
                    dst, sem = rx0(cc, j)
                    push("q", mid, dst, sem, x_peer, "outside")

            def total(tt, j, src):
                s = near_loc[j][0]
                D[cc, tt, s, :, qc] = (
                    P[cc, tt, s].astype(F32) + src[...].astype(F32) + decb_ref[:, bias_cols]
                ).astype(BF16)

            for j in range(2):
                src, sem = rx0(cc, j)
                arrived(src, sem)
                total(0, j, src)
                dec_give(cc, 0, near_loc[j][0], x_peer, "outside")
                dec_give(cc, 0, near_loc[j][0], pair, "outside")
            for j in range(2):
                src, sem = rp(cc, 4 + j)
                arrived(src, sem)
                total(1, j, src)
                dec_give(cc, 1, near_loc[j][0], pair, "outside")
                dec_give(cc, 1, near_loc[j][0], x_peer, "outside")
            for tt in range(2):
                for j in range(2):
                    dec_give_c(cc, tt, near_loc[j][0], "outside")

    def spread_near(cc):
        @pl.when(outside)
        def _():
            for j in range(2):
                s = near_loc[j][1]
                dec_take(cc, 0, s)
                dec_give(cc, 0, s, pair, "outside")
                dec_give_c(cc, 0, s, "outside")

        @pl.when(inside)
        def _():
            for tt, d in ((0, 0), (1, 0), (0, 1)):
                for j in range(2):
                    s = near_loc[j][d]
                    dec_take(cc, tt, s)
                    dec_give(cc, tt, s, inner, "inside")
                    if tt == 1:
                        dec_give(cc, tt, s, x_peer, "inside")
                    dec_give_c(cc, tt, s, "inside")

    def spread_far(cc):
        for tt, d in ((0, 0), (1, 0), (0, 1)):
            for j in range(2):
                s = far_loc[j][d]
                dec_take(cc, tt, s)
                pl.when(inside)(lambda: dec_give(cc, tt, s, pair, "inside"))
                if tt == 1:
                    dec_give(cc, tt, s, x_peer)
                dec_give_c(cc, tt, s)

    def spread_x(cc):
        for locs_of in (near_loc, far_loc):
            for j in range(2):
                s = locs_of[j][1]
                dec_take(cc, 1, s)
                dec_give_c(cc, 1, s)

    def spread_settle(cc):
        for tt in range(2):
            for s in range(locs):
                arrived(D.at[cc, tt, s, :, qo], decc_recv.at[(cc * 2 + tt) * locs + s])

    def latent(cc):
        lg[cc] = jnp.zeros(lg.shape[1:], F32)

        @pl.loop(0, half // tile)
        def _(k):
            cols = pl.ds(pl.multiple_of(k * tile, tile), tile)
            cot = D[cc, :, :, :, cols].astype(F32) - X[cc, :, :, :, cols].astype(F32)
            cot = (cot * cot_scale).astype(BF16)
            C[cc, :, :, :, cols] = cot
            lg[cc] += lax.dot_general(
                cot.reshape(chunk_rows, tile), decw[:, cols],
                (((1,), (1,)), ((), ())), preferred_element_type=F32,
            )
        lg_s[cc] = lg[cc].astype(BF16)
        push("s", lg_s.at[cc], lg_o.at[cc], small_recv.at[4 + cc], y_peer)

    def pre_grad(cc):
        arrived(lg_o.at[cc], small_recv.at[4 + cc])
        pg[part[cc], :] = (
            (lg[cc] + lg_o[cc].astype(F32)) * pre[cc]
        ).astype(BF16)

    push("g", gate.at[t], gate.at[t], small_recv.at[6], y_peer)
    local[1].wait()
    push("f", TY, X.at[c, t, here], y_recv.at[0], y_peer)
    p0, p1, p2, p3 = (0, 0), (0, 1), (1, 0), (1, 1)
    tok_own(p0)

    push("d", decw_hbm.at[:, sent_q], decw_o, small_recv.at[7], c_peer)
    tok_own(p1)
    tok_z(p0, 0)
    tok_x(p0, 0)
    tok_z(p1, 0)
    tok_x(p1, 0)
    tok_own(p2)
    tok_z(p0, 1)
    tok_x(p0, 1)
    tok_z(p1, 1)
    tok_x(p1, 1)
    tok_own(p3)
    tok_z(p0, 2)
    tok_x(p0, 2)
    tok_z(p1, 2)
    tok_x(p1, 2)
    tok_z(p2, 0)
    tok_z(p3, 0)
    tok_x(p0, 3)
    tok_x(p1, 3)
    tok_x(p2, 0)
    tok_x(p3, 0)
    local[2].wait()
    tok_settle(0)
    encode(0)
    tok_z(p2, 1)
    tok_z(p3, 1)
    tok_x(p2, 1)
    tok_x(p3, 1)
    transpose_tokens(0)
    arrived(gate.at[ot], small_recv.at[6])
    activate(0)
    tok_z(p2, 2)
    tok_z(p3, 2)
    tok_x(p2, 2)
    tok_x(p3, 2)
    local[3].wait()
    arrived(decw_o, small_recv.at[7])
    decode(0)
    sum_start(0)
    tok_x(p2, 3)
    tok_x(p3, 3)
    tok_settle(1)
    encode(1)
    sum_far(0)
    activate(1)
    sum_near(0)
    decode(1)
    sum_start(1)
    sum_last(0)
    slopes(0)
    transpose_tokens(1)
    sum_far(1)
    spread_near(0)
    sum_near(1)
    slopes(1)
    spread_far(0)
    sum_last(1)
    spread_x(0)
    spread_settle(0)
    latent(0)
    spread_near(1)
    spread_far(1)
    spread_x(1)
    spread_settle(1)
    latent(1)
    push("f", D.at[c, ot, here], RY, y_recv.at[1], y_peer)
    out = [pltpu.make_async_copy(D.at[c, t, here], recon_ref.at[:, mine], local_sem.at[4])]
    out[0].start()
    tile_o = 512
    steps = half // tile_o
    for k in range(steps):
        cols = slice(k * tile_o, (k + 1) * tile_o)
        dg[:, cols] = jnp.dot(
            act_t[...], C[:, :, :, :, cols].reshape(2 * chunk_rows, tile_o),
            preferred_element_type=F32,
        ).astype(BF16)
        out.append(pltpu.make_async_copy(dg.at[:, cols], decg_ref.at[:, cols], out_sem.at[k]))
        out[-1].start()
    pre_grad(0)
    finish_sends()
    arrived(RY, y_recv.at[1])
    out.append(pltpu.make_async_copy(RY, recon_ref.at[:, theirs], local_sem.at[5]))
    out[-1].start()
    pre_grad(1)
    for k in range(steps):
        cols = slice(k * tile_o, (k + 1) * tile_o)
        eg[cols, :] = jnp.dot(
            XT[cols, :], pg[...], preferred_element_type=F32
        ).astype(BF16)
        out.append(
            pltpu.make_async_copy(eg.at[cols], encg_ref.at[cols], out_sem.at[steps + k])
        )
        out[-1].start()
    for copy in out:
        copy.wait()


def fused_shards(tokens, enc_weight, enc_bias, dec_weight, dec_bias, active_blocks):
    rows, width = tokens.shape
    lat_count = lax.axis_size("lat")
    tok_count = lax.axis_size("tok")
    group_rows = rows * lat_count
    latents = enc_weight.shape[1]
    half = width // tok_count
    quarter = half // NC
    locs = lat_count // NC
    chunk_rows = 2 * locs * rows
    blocks = active_blocks.shape[0]
    cot_scale = 1.0 / math.sqrt(group_rows * tok_count)
    hbm = pl.BlockSpec(memory_space=pl.ANY)
    vmem = pl.BlockSpec(memory_space=pltpu.VMEM)
    dma = pltpu.SemaphoreType.DMA
    pieces = pltpu.VMEM((2, 2, locs, rows, half), BF16)
    small = pltpu.VMEM((2, chunk_rows, latents), BF16)
    small_f = pltpu.VMEM((2, chunk_rows, latents), F32)

    def slots(n):
        return pltpu.VMEM((2, n, rows, quarter), BF16)

    recon, encg, decg = pl.pallas_call(
        functools.partial(fused_kernel, cot_scale),
        out_shape=(
            jax.ShapeDtypeStruct((rows, width), BF16),
            jax.ShapeDtypeStruct((half, latents), BF16),
            jax.ShapeDtypeStruct((latents, half), BF16),
        ),
        in_specs=[hbm, hbm, vmem, hbm, vmem, pl.BlockSpec(memory_space=pltpu.SMEM)],
        out_specs=(hbm, hbm, hbm),
        scratch_shapes=[
            pltpu.VMEM((half, latents), BF16),
            pltpu.VMEM((latents, half), BF16),
            pltpu.VMEM((latents, quarter), BF16),
            pltpu.VMEM((rows, half), BF16),
            pltpu.VMEM((rows, half), BF16),
            pieces,
            pltpu.VMEM((half, 2 * chunk_rows), BF16),
            pieces,
            pieces,
            pltpu.VMEM((2, 2, locs, rows, quarter), BF16),
            slots(4), slots(2), slots(6), slots(6),
            small_f, small, small, small, small,
            pltpu.VMEM((latents, 2 * chunk_rows), BF16),
            small_f, small, small,
            pltpu.VMEM((2 * chunk_rows, latents), BF16),
            pltpu.VMEM((tok_count, blocks, 8, latents), F32),
            pltpu.VMEM((half, latents), BF16),
            pltpu.VMEM((latents, half), BF16),
            dma((6,)), dma((16,)), dma((320,)), dma((2,)),
            dma((32,)), dma((32,)), dma((32,)), dma((32,)),
            dma((8,)), dma((4,)), dma((12,)), dma((12,)), dma((8,)),
        ],
        compiler_params=pltpu.CompilerParams(
            collective_id=0, has_side_effects=True, vmem_limit_bytes=48 * 1024 * 1024
        ),
        name="fused_step",
    )(tokens, enc_weight, enc_bias[None, :], dec_weight, dec_bias[None, :], active_blocks)
    return recon, encg.astype(F32), decg.astype(F32)


def shards(tokens, enc_weight, enc_bias, dec_weight, dec_bias, active_blocks):
    tok_dev = tokens.shape[0]
    lat_count = lax.axis_size("lat")
    tok_count = lax.axis_size("tok")
    group_rows = tok_dev * lat_count
    latent_width = enc_weight.shape[1]
    block_count = active_blocks.shape[0]
    block_rows = group_rows // block_count
    blocks_here = latent_width // LB
    owner_index = lax.axis_index("lat")
    cot_scale = 1.0 / math.sqrt(group_rows * tok_count)
    block_ids = owner_index * blocks_here + jnp.arange(blocks_here, dtype=jnp.int32)
    block_hits = jnp.any(active_blocks[:, :, None] == block_ids[None, None, :], axis=1).astype(
        jnp.float32
    )
    latent_gate = jnp.repeat(block_hits, LB, axis=1)[:, None, :]
    bias_row = enc_bias[None, None, :]
    gathered = lax.all_gather(tokens, "lat", axis=0, tiled=True)
    pre_act = (
        jnp.dot(gathered, enc_weight, preferred_element_type=jnp.float32).reshape(
            block_count, block_rows, latent_width
        )
        + bias_row
    )
    activations = (
        (jax.nn.silu(pre_act) * latent_gate).astype(jnp.bfloat16).reshape(group_rows, latent_width)
    )
    bias_dec = dec_bias[None, :]
    partial_sum = jnp.dot(activations, dec_weight, preferred_element_type=jnp.float32)
    decoded_all = lax.psum(partial_sum.astype(jnp.bfloat16), "lat").astype(jnp.float32) + bias_dec
    cot_all = ((decoded_all - gathered.astype(jnp.float32)) * cot_scale).astype(jnp.bfloat16)
    decoded = lax.dynamic_slice_in_dim(decoded_all, owner_index * tok_dev, tok_dev, 0)
    dec_local = contract_rows(activations, cot_all)
    latent_grad = lax.dot_general(
        cot_all, dec_weight, (((1,), (1,)), ((), ())), preferred_element_type=jnp.float32
    )
    sigma = jax.nn.sigmoid(pre_act)
    slope = sigma * (1.0 + pre_act * (1.0 - sigma))
    pre_grad = (
        (latent_grad.reshape(block_count, block_rows, latent_width) * slope * latent_gate)
        .astype(jnp.bfloat16)
        .reshape(group_rows, latent_width)
    )
    enc_local = contract_rows(gathered, pre_grad)
    enc_grad, dec_grad = (
        lax.psum_scatter(
            enc_local.astype(jnp.bfloat16), "tok", scatter_dimension=0, tiled=True
        ).astype(jnp.float32),
        lax.psum_scatter(
            dec_local.astype(jnp.bfloat16), "tok", scatter_dimension=1, tiled=True
        ).astype(jnp.float32),
    )
    return (decoded.astype(jnp.bfloat16), enc_grad, dec_grad)


def solution(mesh):
    placed = (
        P(("tok", "lat"), None),
        P(None, "lat"),
        P("lat"),
        P("lat", None),
        P(),
        P("tok", None),
    )
    fits = mesh.shape["tok"] == 2 and mesh.shape["lat"] == NZ * NX * NC
    return jax.shard_map(
        fused_shards if fits else shards,
        mesh=mesh,
        in_specs=placed,
        out_specs=(P(("tok", "lat"), None), P("tok", "lat"), P("lat", "tok")),
        check_vma=False,
    )
```

```python
import functools
import math

import jax
import jax.numpy as jnp
from jax import lax
from jax.experimental import pallas as pl
from jax.experimental.pallas import tpu as pltpu
from jax.sharding import PartitionSpec as P

LB = 256
MESH = pl.DeviceIdType.MESH
NZ, NX, NC = 4, 2, 2
Z_ORDER = (2, 1, 3)
BF16 = jnp.bfloat16
F32 = jnp.float32


def contract_rows(left_rows, right_rows):
    return lax.dot_general(
        left_rows, right_rows, (((0,), (0,)), ((), ())), preferred_element_type=jnp.float32
    )


def fused_kernel(
    cot_scale,
    tok_hbm, encw_hbm, encb_hbm, decw_hbm, decb_hbm, blocks_hbm,
    recon_ref, XT, pg, dg,
    encw, decw, decw_o, encb, decb, YQ, RY, X, D, C, P, RX, RZ,
    pre, pre_s, pre_o, act, act_o, act_t, lg, lg_s, lg_o, gate, blocks_ref,
    local_sem, send_sem, y_recv, own_recv, tok_recv, tokc_recv, dec_recv, decc_recv,
    rx_recv, rz_recv, small_recv,
):
    t = lax.axis_index("tok")
    l = lax.axis_index("lat")
    z, x, c = l // (NX * NC), (l // NC) % NX, l % NC
    rows, width = tok_hbm.shape
    half = width // 2
    quarter = half // 2
    locs = NZ * NX
    chunk_rows = 2 * locs * rows
    latents = encw.shape[1]

    ox, ot = 1 - x, 1 - t
    pair_z = z + 1 - 2 * lax.rem(z, 2)
    near = z // 2
    sources = (pair_z, 2 - near, 3 - 3 * near)
    ring = [lax.rem(z + dz, NZ) for dz in Z_ORDER]
    inside = jnp.logical_and(z >= 1, z <= 2)

    def place(zz, xx):
        return (zz * NX + xx) * NC + c

    pair = (t, place(pair_z, x))
    inner = (t, place(3 - z, x))
    z_peer = [(t, place(zz, x)) for zz in ring]
    x_peer = (t, place(z, ox))
    c_peer = (t, (z * NX + x) * NC + 1 - c)
    y_peer = (ot, l)

    mine = pl.ds(pl.multiple_of(t * half, half), half)
    theirs = pl.ds(pl.multiple_of(ot * half, half), half)
    qc = pl.ds(pl.multiple_of(c * quarter, quarter), quarter)
    qo = pl.ds(pl.multiple_of((1 - c) * quarter, quarter), quarter)
    sent_q = pl.ds(pl.multiple_of(t * half + (1 - c) * quarter, quarter), quarter)

    own_q = pl.ds(pl.multiple_of(t * half + c * quarter, quarter), quarter)
    y_own_q = pl.ds(pl.multiple_of(ot * half + c * quarter, quarter), quarter)
    y_sent_q = pl.ds(pl.multiple_of(ot * half + (1 - c) * quarter, quarter), quarter)

    local = [
        pltpu.make_async_copy(tok_hbm.at[:, own_q], X.at[c, t, z, x, :, qc], local_sem.at[0]),
        pltpu.make_async_copy(encw_hbm.at[mine], encw, local_sem.at[1]),
        pltpu.make_async_copy(decw_hbm.at[:, mine], decw, local_sem.at[2]),
        pltpu.make_async_copy(encb_hbm, encb, local_sem.at[3]),
        pltpu.make_async_copy(decb_hbm.at[:, own_q], decb, local_sem.at[4]),
        pltpu.make_async_copy(blocks_hbm, blocks_ref, local_sem.at[5]),
    ]
    for copy in local:
        copy.start()

    block_count = blocks_ref.shape[0]
    barrier = pltpu.get_barrier_semaphore()
    for peer in (pair, x_peer, c_peer, y_peer):
        pl.semaphore_signal(barrier, inc=1, device_id=peer, device_id_type=MESH)

    @pl.when(inside)
    def _():
        pl.semaphore_signal(barrier, inc=1, device_id=inner, device_id_type=MESH)
        pl.semaphore_wait(barrier, 5)

    @pl.when(jnp.logical_not(inside))
    def _():
        pl.semaphore_wait(barrier, 4)

    flags = {"inside": inside, "c0": c == 0, "c1": c == 1}
    sems = [0]
    batches = []

    def push(kind, src, dst, recv, peer, who="all"):
        for batch in batches:
            if batch[0] == (kind, who) and kind == "q" and batch[2] < NZ:
                break
        else:
            batch = [(kind, who), sems[0], 0]
            batches.append(batch)
            sems[0] += 1
        batch[2] += 1
        pltpu.make_async_remote_copy(
            src_ref=src, dst_ref=dst, send_sem=send_sem.at[batch[1]], recv_sem=recv,
            device_id=peer, device_id_type=MESH,
        ).start()

    def arrived(dst, recv):
        pltpu.make_async_remote_copy(
            src_ref=dst, dst_ref=dst, send_sem=send_sem.at[0], recv_sem=recv,
            device_id=c_peer, device_id_type=MESH,
        ).wait_recv()

    def finish_sends():
        shape_of = {"f": RY, "s": act.at[0], "d": decw_o, "g": gate.at[0], "h": act.at[0, :chunk_rows // 2], "e": P.at[0, 0, :, 0]}

        def wait(kind, sem, n):
            ref = RZ.at[0, 0, :n] if kind == "q" else shape_of[kind]
            pltpu.make_async_remote_copy(
                src_ref=ref, dst_ref=ref, send_sem=send_sem.at[sem],
                recv_sem=small_recv.at[0], device_id=c_peer, device_id_type=MESH,
            ).wait_send()

        for who in ("all",) + tuple(flags):
            items = [(kind, sem, n) for (kind, w), sem, n in batches if w == who]

            def go():
                for item in items:
                    wait(*item)
            if who == "all":
                go()
            elif items:
                pl.when(flags[who])(go)

    def group_of(k):
        return t if k == 0 else ot

    class Gather:
        def __init__(self, full, recv, core_recv, group):
            self.full, self.recv, self.core_recv, self.group = full, recv, core_recv, group

        def ref(self, p, zz, xx):
            cc, k = p
            tt = self.group(k)
            sem = self.recv.at[((cc * 2 + tt) * NZ + zz) * NX + xx]
            return self.full.at[cc, tt, zz, xx, :, qc], sem

        def give(self, p, zz, xx, peer, who="all"):
            ref, sem = self.ref(p, zz, xx)
            push("q", ref, ref, sem, peer, who)

        def own(self, p):
            self.give(p, z, x, pair)
            self.give(p, z, x, x_peer)
            pl.when(inside)(lambda: self.give(p, z, x, inner, "inside"))

        def along_z(self, p, i):
            zz = sources[i]
            arrived(*self.ref(p, zz, x))
            to = inner if i == 0 else pair
            pl.when(inside)(lambda: self.give(p, zz, x, to, "inside"))
            self.give(p, zz, x, x_peer)

        def to_core(self, p, xx, slot):
            cc, k = p
            tt = self.group(k)
            ref = self.full.at[cc, tt, :, xx, :, qc]
            push("e", ref, ref, self.core_recv.at[(cc * 2 + tt) * 2 + slot], c_peer)

        def line(self, p):
            self.to_core(p, x, 0)

        def cross(self, p):
            for zz in (z,) + sources:
                arrived(*self.ref(p, zz, ox))
            self.to_core(p, ox, 1)

        def settle(self, cc, groups=(0, 1)):
            for tt in groups:
                for slot, xx in enumerate((x, ox)):
                    arrived(
                        self.full.at[cc, tt, :, xx, :, qo],
                        self.core_recv.at[(cc * 2 + tt) * 2 + slot],
                    )

    toks = Gather(X, tok_recv, tokc_recv, group_of)
    decs = Gather(D, dec_recv, decc_recv, lambda k: k)

    def tok_own(p):
        cc, k = p
        tt = group_of(k)
        own_sem = own_recv.at[cc * 2 + k]

        @pl.when(c == cc)
        def _():
            src = tok_hbm.at[:, sent_q] if k == 0 else YQ
            if k == 1:
                arrived(YQ, y_recv.at[1])
            push("q", src, X.at[cc, tt, z, x, :, qo], own_sem, c_peer, f"c{cc}")
            if k == 0:
                local[0].wait()
            else:
                arrived(X.at[cc, tt, z, x, :, qc], y_recv.at[0])

        @pl.when(c != cc)
        def _():
            arrived(X.at[cc, tt, z, x, :, qc], own_sem)

        toks.own(p)

    part = [pl.ds(cc * chunk_rows, chunk_rows) for cc in range(2)]
    tile = 1024

    def encode(cc):
        pre[cc] = jnp.dot(
            X[cc, :, :, :, :, :tile].reshape(chunk_rows, tile), encw[:tile, :],
            preferred_element_type=F32,
        )

        @pl.loop(1, half // tile)
        def _(k):
            cols = pl.ds(pl.multiple_of(k * tile, tile), tile)
            pre[cc] += jnp.dot(
                X[cc, :, :, :, :, cols].reshape(chunk_rows, tile), encw[cols, :],
                preferred_element_type=F32,
            )
        pre_s[cc] = pre[cc].astype(BF16)
        push("s", pre_s.at[cc], pre_o.at[cc], small_recv.at[cc], y_peer)

    tile_t = 512

    def transpose_tokens(cc):
        @pl.loop(0, half // tile_t)
        def _(k):
            cols = pl.ds(pl.multiple_of(k * tile_t, tile_t), tile_t)
            XT[cols, part[cc]] = X[cc, :, :, :, :, cols].reshape(chunk_rows, tile_t).T

    seg_rows = locs * rows // block_count

    def segments():
        for tt in range(2):
            for b in range(block_count):
                at = (tt * block_count + b) * seg_rows
                yield slice(at, at + seg_rows), gate[tt, b][:1, :]

    def activate(cc):
        arrived(pre_o.at[cc], small_recv.at[cc])
        for seg, g in segments():
            v = pre[cc, seg, :] + pre_o[cc, seg, :].astype(F32) + encb[...]
            pre[cc, seg, :] = v
            act[cc, seg, :] = (v * jax.nn.sigmoid(v) * g).astype(BF16)
        push("s", act.at[cc], act_o.at[cc], small_recv.at[2 + cc], c_peer)

    def slopes(cc):
        act_t[:, part[cc]] = act[cc].T
        for seg, g in segments():
            v = pre[cc, seg, :]
            sigma = jax.nn.sigmoid(v)
            pre[cc, seg, :] = sigma * (1.0 + v * (1.0 - sigma)) * g

    tile_d = 512

    def decode(cc):
        arrived(act_o.at[cc], small_recv.at[2 + cc])

        @pl.loop(0, quarter // tile_d)
        def _(k):
            cols = pl.ds(pl.multiple_of(k * tile_d, tile_d), tile_d)
            own_cols = pl.ds(pl.multiple_of(c * quarter + k * tile_d, tile_d), tile_d)
            term = jnp.dot(act[cc], decw[:, own_cols], preferred_element_type=F32)
            term = term + jnp.dot(act_o[cc], decw_o[:, cols], preferred_element_type=F32)
            P[cc, :, :, :, :, cols] = term.astype(BF16).reshape(2, NZ, NX, rows, tile_d)

    def add(dst, *terms):
        total = dst[...].astype(F32)
        for other in terms:
            total = total + other[...].astype(F32)
        dst[...] = total.astype(BF16)

    def sum_x(cc):
        for zz in ring + [z]:
            for tt in range(2):
                    push(
                    "q", P.at[cc, tt, zz, ox], RX.at[cc, tt, zz],
                    rx_recv.at[(cc * 2 + tt) * NZ + zz], x_peer,
                )

    def sum_z(cc, i):
        zz = ring[i]
        for tt in range(2):
            mid = P.at[cc, tt, zz, x]
            arrived(RX.at[cc, tt, zz], rx_recv.at[(cc * 2 + tt) * NZ + zz])
            add(mid, RX.at[cc, tt, zz])
            push("q", mid, RZ.at[cc, tt, z], rz_recv.at[(cc * 2 + tt) * NZ + z], z_peer[i])

    def sum_own(cc):
        for tt in range(2):
            arrived(RX.at[cc, tt, z], rx_recv.at[(cc * 2 + tt) * NZ + z])
            for zz in sources:
                arrived(RZ.at[cc, tt, zz], rz_recv.at[(cc * 2 + tt) * NZ + zz])
            total = P[cc, tt, z, x].astype(F32) + RX[cc, tt, z].astype(F32)
            for zz in sources:
                total = total + RZ[cc, tt, zz].astype(F32)
            D[cc, tt, z, x, :, qc] = (total + decb[...]).astype(BF16)
            decs.own((cc, tt))

    def rows_of(cc, tt):
        at = cc * chunk_rows + tt * (chunk_rows // 2)
        return slice(at, at + chunk_rows // 2)

    def latent(cc, tt):
        decs.settle(cc, (tt,))
        sub = slice(tt * (chunk_rows // 2), (tt + 1) * (chunk_rows // 2))
        lg[cc, sub, :] = jnp.zeros((chunk_rows // 2, latents), F32)

        @pl.loop(0, half // tile)
        def _(k):
            cols = pl.ds(pl.multiple_of(k * tile, tile), tile)
            cot = D[cc, tt, :, :, :, cols].astype(F32) - X[cc, tt, :, :, :, cols].astype(F32)
            cot = (cot * cot_scale).astype(BF16)
            C[cc, tt, :, :, :, cols] = cot
            lg[cc, sub, :] += lax.dot_general(
                cot.reshape(chunk_rows // 2, tile), decw[:, cols],
                (((1,), (1,)), ((), ())), preferred_element_type=F32,
            )
        lg_s[cc, sub, :] = lg[cc, sub, :].astype(BF16)
        push(
            "h", lg_s.at[cc, sub], lg_o.at[cc, sub], small_recv.at[8 + cc * 2 + tt], y_peer
        )

    def pre_grad(cc, tt):
        sub = slice(tt * (chunk_rows // 2), (tt + 1) * (chunk_rows // 2))
        arrived(lg_o.at[cc, sub], small_recv.at[8 + cc * 2 + tt])
        pg[rows_of(cc, tt), :] = (
            (lg[cc, sub, :] + lg_o[cc, sub, :].astype(F32)) * pre[cc, sub, :]
        ).astype(BF16)

    push("q", tok_hbm.at[:, y_own_q], X.at[c, t, z, x, :, qc], y_recv.at[0], y_peer)
    push("q", tok_hbm.at[:, y_sent_q], YQ, y_recv.at[1], y_peer)
    p0, p1, p2, p3 = (0, 0), (0, 1), (1, 0), (1, 1)
    tok_own(p0)
    local[5].wait()
    for b in range(block_count):
        hit = blocks_ref[b, 0] == l
        for slot in range(1, blocks_ref.shape[1]):
            hit = jnp.logical_or(hit, blocks_ref[b, slot] == l)
        gate[t, b] = jnp.broadcast_to(jnp.where(hit, 1.0, 0.0).astype(F32), gate.shape[2:])
    push("g", gate.at[t], gate.at[t], small_recv.at[6], y_peer)
    tok_own(p1)
    push("d", decw_hbm.at[:, sent_q], decw_o, small_recv.at[7], c_peer)
    toks.along_z(p0, 0)
    toks.along_z(p1, 0)
    tok_own(p2)
    toks.along_z(p0, 1)
    toks.along_z(p1, 1)
    tok_own(p3)
    toks.along_z(p0, 2)
    toks.line(p0)
    toks.along_z(p1, 2)
    toks.line(p1)
    toks.along_z(p2, 0)
    toks.cross(p0)
    toks.along_z(p3, 0)
    toks.cross(p1)
    local[1].wait()
    toks.settle(0)
    encode(0)
    toks.along_z(p2, 1)
    toks.along_z(p3, 1)
    transpose_tokens(0)
    local[3].wait()
    arrived(gate.at[ot], small_recv.at[6])
    activate(0)
    toks.along_z(p2, 2)
    toks.line(p2)
    toks.along_z(p3, 2)
    toks.line(p3)
    local[2].wait()
    arrived(decw_o, small_recv.at[7])
    decode(0)
    sum_x(0)
    local[4].wait()
    toks.cross(p2)
    toks.cross(p3)
    toks.settle(1)
    encode(1)
    sum_z(0, 0)
    sum_z(0, 1)
    sum_z(0, 2)
    activate(1)
    slopes(0)
    decode(1)
    sum_x(1)
    sum_own(0)
    sum_z(1, 0)
    decs.along_z(p0, 0)
    decs.along_z(p1, 0)
    sum_z(1, 1)
    decs.along_z(p0, 1)
    decs.along_z(p1, 1)
    sum_z(1, 2)
    decs.along_z(p0, 2)
    decs.line(p0)
    decs.along_z(p1, 2)
    decs.line(p1)
    transpose_tokens(1)
    slopes(1)
    sum_own(1)
    decs.along_z(p2, 0)
    decs.along_z(p3, 0)
    decs.cross(p0)
    decs.cross(p1)
    decs.along_z(p2, 1)
    decs.along_z(p3, 1)
    latent(0, 0)
    latent(0, 1)
    decs.along_z(p2, 2)
    decs.line(p2)
    decs.along_z(p3, 2)
    decs.line(p3)
    pre_grad(0, 0)
    pre_grad(0, 1)
    decs.cross(p2)
    latent(1, 0)
    decs.cross(p3)
    latent(1, 1)
    push("f", D.at[c, ot, z, x], RY, y_recv.at[2], y_peer)
    tile_o = 512

    @pl.loop(0, half // tile_o)
    def _(k):
        cols = pl.ds(pl.multiple_of(k * tile_o, tile_o), tile_o)
        dg[:, cols] = jnp.dot(
            act_t[...], C[:, :, :, :, :, cols].reshape(2 * chunk_rows, tile_o),
            preferred_element_type=F32,
        )
    recon_ref[:, mine] = D[c, t, z, x]
    pre_grad(1, 0)
    finish_sends()
    pre_grad(1, 1)
    arrived(RY, y_recv.at[2])
    recon_ref[:, theirs] = RY[...]


def grads_kernel(recon_in, xt, pg, dg, recon_out, encg_out, decg_out, eg, sems):
    copies = [
        pltpu.make_async_copy(dg, decg_out, sems.at[0]),
        pltpu.make_async_copy(recon_in, recon_out, sems.at[1]),
    ]
    for copy in copies:
        copy.start()
    tile = 512
    for k in range(xt.shape[0] // tile):
        cols = slice(k * tile, (k + 1) * tile)
        eg[cols, :] = jnp.dot(xt[cols, :], pg[...], preferred_element_type=F32)
        copies.append(
            pltpu.make_async_copy(eg.at[cols], encg_out.at[cols], sems.at[2 + k])
        )
        copies[-1].start()
    for copy in copies:
        copy.wait()


def fused_shards(tokens, enc_weight, enc_bias, dec_weight, dec_bias, active_blocks):
    rows, width = tokens.shape
    lat_count = lax.axis_size("lat")
    tok_count = lax.axis_size("tok")
    group_rows = rows * lat_count
    latents = enc_weight.shape[1]
    half = width // tok_count
    quarter = half // NC
    locs = lat_count // NC
    chunk_rows = 2 * locs * rows
    blocks = active_blocks.shape[0]
    cot_scale = 1.0 / math.sqrt(group_rows * tok_count)
    hbm = pl.BlockSpec(memory_space=pltpu.HBM)
    vmem = pl.BlockSpec(memory_space=pltpu.VMEM)
    dma = pltpu.SemaphoreType.DMA
    pieces = pltpu.VMEM((2, 2, NZ, NX, rows, half), BF16)
    small = pltpu.VMEM((2, chunk_rows, latents), BF16)
    small_f = pltpu.VMEM((2, chunk_rows, latents), F32)

    slots = pltpu.VMEM((2, 2, NZ, rows, quarter), BF16)
    inputs = [
        pltpu.with_memory_space_constraint(a, pltpu.HBM)
        for a in (
            tokens, enc_weight, enc_bias[None, :], dec_weight, dec_bias[None, :], active_blocks
        )
    ]
    recon, xt, pg, dg = pl.pallas_call(
        functools.partial(fused_kernel, cot_scale),
        out_shape=(
            jax.ShapeDtypeStruct((rows, width), BF16),
            jax.ShapeDtypeStruct((half, 2 * chunk_rows), BF16),
            jax.ShapeDtypeStruct((2 * chunk_rows, latents), BF16),
            jax.ShapeDtypeStruct((latents, half), F32),
        ),
        in_specs=[hbm] * 6,
        out_specs=(vmem,) * 4,
        scratch_shapes=[
            pltpu.VMEM((half, latents), BF16),
            pltpu.VMEM((latents, half), BF16),
            pltpu.VMEM((latents, quarter), BF16),
            pltpu.VMEM((1, latents), F32),
            pltpu.VMEM((1, quarter), F32),
            pltpu.VMEM((rows, quarter), BF16),
            pltpu.VMEM((rows, half), BF16),
            pieces,
            pieces,
            pieces,
            pltpu.VMEM((2, 2, NZ, NX, rows, quarter), BF16),
            slots, slots,
            small_f, small, small, small, small,
            pltpu.VMEM((latents, 2 * chunk_rows), BF16),
            small_f, small, small,
            pltpu.VMEM((tok_count, blocks, 8, latents), F32),
            pltpu.SMEM(active_blocks.shape, jnp.int32),
            dma((6,)), dma((80,)), dma((3,)), dma((4,)),
            dma((32,)), dma((8,)), dma((32,)), dma((8,)),
            dma((16,)), dma((16,)), dma((12,)),
        ],
        compiler_params=pltpu.CompilerParams(
            collective_id=0, has_side_effects=True, vmem_limit_bytes=40 * 1024 * 1024
        ),
        name="fused_step",
    )(*inputs)
    return pl.pallas_call(
        grads_kernel,
        out_shape=(
            jax.ShapeDtypeStruct((rows, width), BF16),
            jax.ShapeDtypeStruct((half, latents), F32),
            jax.ShapeDtypeStruct((latents, half), F32),
        ),
        in_specs=[vmem] * 4,
        out_specs=(hbm,) * 3,
        scratch_shapes=[pltpu.VMEM((half, latents), F32), dma((2 + half // 512,))],
        compiler_params=pltpu.CompilerParams(vmem_limit_bytes=16 * 1024 * 1024),
        name="weight_grads",
    )(recon, xt, pg, dg)


def shards(tokens, enc_weight, enc_bias, dec_weight, dec_bias, active_blocks):
    tok_dev = tokens.shape[0]
    lat_count = lax.axis_size("lat")
    tok_count = lax.axis_size("tok")
    group_rows = tok_dev * lat_count
    latent_width = enc_weight.shape[1]
    block_count = active_blocks.shape[0]
    block_rows = group_rows // block_count
    blocks_here = latent_width // LB
    owner_index = lax.axis_index("lat")
    cot_scale = 1.0 / math.sqrt(group_rows * tok_count)
    block_ids = owner_index * blocks_here + jnp.arange(blocks_here, dtype=jnp.int32)
    block_hits = jnp.any(active_blocks[:, :, None] == block_ids[None, None, :], axis=1).astype(
        jnp.float32
    )
    latent_gate = jnp.repeat(block_hits, LB, axis=1)[:, None, :]
    bias_row = enc_bias[None, None, :]
    gathered = lax.all_gather(tokens, "lat", axis=0, tiled=True)
    pre_act = (
        jnp.dot(gathered, enc_weight, preferred_element_type=jnp.float32).reshape(
            block_count, block_rows, latent_width
        )
        + bias_row
    )
    activations = (
        (jax.nn.silu(pre_act) * latent_gate).astype(jnp.bfloat16).reshape(group_rows, latent_width)
    )
    bias_dec = dec_bias[None, :]
    partial_sum = jnp.dot(activations, dec_weight, preferred_element_type=jnp.float32)
    decoded_all = lax.psum(partial_sum.astype(jnp.bfloat16), "lat").astype(jnp.float32) + bias_dec
    cot_all = ((decoded_all - gathered.astype(jnp.float32)) * cot_scale).astype(jnp.bfloat16)
    decoded = lax.dynamic_slice_in_dim(decoded_all, owner_index * tok_dev, tok_dev, 0)
    dec_local = contract_rows(activations, cot_all)
    latent_grad = lax.dot_general(
        cot_all, dec_weight, (((1,), (1,)), ((), ())), preferred_element_type=jnp.float32
    )
    sigma = jax.nn.sigmoid(pre_act)
    slope = sigma * (1.0 + pre_act * (1.0 - sigma))
    pre_grad = (
        (latent_grad.reshape(block_count, block_rows, latent_width) * slope * latent_gate)
        .astype(jnp.bfloat16)
        .reshape(group_rows, latent_width)
    )
    enc_local = contract_rows(gathered, pre_grad)
    enc_grad, dec_grad = (
        lax.psum_scatter(
            enc_local.astype(jnp.bfloat16), "tok", scatter_dimension=0, tiled=True
        ).astype(jnp.float32),
        lax.psum_scatter(
            dec_local.astype(jnp.bfloat16), "tok", scatter_dimension=1, tiled=True
        ).astype(jnp.float32),
    )
    return (decoded.astype(jnp.bfloat16), enc_grad, dec_grad)


def solution(mesh):
    placed = (
        P(("tok", "lat"), None),
        P(None, "lat"),
        P("lat"),
        P("lat", None),
        P(),
        P("tok", None),
    )
    fits = mesh.shape["tok"] == 2 and mesh.shape["lat"] == NZ * NX * NC
    return jax.shard_map(
        fused_shards if fits else shards,
        mesh=mesh,
        in_specs=placed,
        out_specs=(P(("tok", "lat"), None), P("tok", "lat"), P("lat", "tok")),
        check_vma=False,
    )
```

```python
import functools
import math

import jax
import jax.numpy as jnp
from jax import lax
from jax.experimental import pallas as pl
from jax.experimental.pallas import tpu as pltpu
from jax.sharding import PartitionSpec as P

LB = 256
MESH = pl.DeviceIdType.MESH
NZ, NX, NC = 4, 2, 2
Z_ORDER = (2, 1, 3)
BF16 = jnp.bfloat16
F32 = jnp.float32


def contract_rows(left_rows, right_rows):
    return lax.dot_general(
        left_rows, right_rows, (((0,), (0,)), ((), ())), preferred_element_type=jnp.float32
    )


def fused_kernel(
    cot_scale,
    tok_hbm, encw_hbm, encb_hbm, decw_hbm, decb_hbm, blocks_hbm,
    recon_ref, XT, pg, dg,
    encw, decw, decw_o, encb, decb, YQ, RY, X, D, C, P, RX, RZ, RP,
    pre, pre_s, pre_o, act, act_o, act_t, lg, lg_s, lg_o, lgp, lgp_s, lgp_o, gate, blocks_ref,
    local_sem, send_sem, y_recv, own_recv, tok_recv, tokc_recv, dec_recv, decc_recv,
    rx_recv, rz_recv, rp_recv, small_recv,
):
    t = lax.axis_index("tok")
    l = lax.axis_index("lat")
    z, x, c = l // (NX * NC), (l // NC) % NX, l % NC
    rows, width = tok_hbm.shape
    half = width // 2
    quarter = half // 2
    locs = NZ * NX
    chunk_rows = 2 * locs * rows
    latents = encw.shape[1]

    ox, ot = 1 - x, 1 - t
    pair_z = z + 1 - 2 * lax.rem(z, 2)
    near = z // 2
    sources = (pair_z, 2 - near, 3 - 3 * near)
    ring = [lax.rem(z + dz, NZ) for dz in Z_ORDER]
    inside = jnp.logical_and(z >= 1, z <= 2)

    def place(zz, xx):
        return (zz * NX + xx) * NC + c

    pair = (t, place(pair_z, x))
    inner = (t, place(3 - z, x))
    x_peer = (t, place(z, ox))
    c_peer = (t, (z * NX + x) * NC + 1 - c)
    y_peer = (ot, l)

    mine = pl.ds(pl.multiple_of(t * half, half), half)
    theirs = pl.ds(pl.multiple_of(ot * half, half), half)
    qc = pl.ds(pl.multiple_of(c * quarter, quarter), quarter)
    qo = pl.ds(pl.multiple_of((1 - c) * quarter, quarter), quarter)
    sent_q = pl.ds(pl.multiple_of(t * half + (1 - c) * quarter, quarter), quarter)

    own_q = pl.ds(pl.multiple_of(t * half + c * quarter, quarter), quarter)
    y_own_q = pl.ds(pl.multiple_of(ot * half + c * quarter, quarter), quarter)
    y_sent_q = pl.ds(pl.multiple_of(ot * half + (1 - c) * quarter, quarter), quarter)

    local = [
        pltpu.make_async_copy(tok_hbm.at[:, own_q], X.at[c, t, z, x, :, qc], local_sem.at[0]),
        pltpu.make_async_copy(encw_hbm.at[mine], encw, local_sem.at[1]),
        pltpu.make_async_copy(decw_hbm.at[:, mine], decw, local_sem.at[2]),
        pltpu.make_async_copy(encb_hbm, encb, local_sem.at[3]),
        pltpu.make_async_copy(decb_hbm.at[:, own_q], decb, local_sem.at[4]),
        pltpu.make_async_copy(blocks_hbm, blocks_ref, local_sem.at[5]),
    ]
    for copy in local:
        copy.start()

    block_count = blocks_ref.shape[0]
    barrier = pltpu.get_barrier_semaphore()
    for peer in (pair, x_peer, c_peer, y_peer):
        pl.semaphore_signal(barrier, inc=1, device_id=peer, device_id_type=MESH)

    @pl.when(inside)
    def _():
        pl.semaphore_signal(barrier, inc=1, device_id=inner, device_id_type=MESH)
        pl.semaphore_wait(barrier, 5)

    @pl.when(jnp.logical_not(inside))
    def _():
        pl.semaphore_wait(barrier, 4)

    flags = {"inside": inside, "c0": c == 0, "c1": c == 1}
    sems = [0]
    batches = []

    def push(kind, src, dst, recv, peer, who="all"):
        for batch in batches:
            if batch[0] == (kind, who) and kind == "q" and batch[2] < NZ:
                break
        else:
            batch = [(kind, who), sems[0], 0]
            batches.append(batch)
            sems[0] += 1
        batch[2] += 1
        pltpu.make_async_remote_copy(
            src_ref=src, dst_ref=dst, send_sem=send_sem.at[batch[1]], recv_sem=recv,
            device_id=peer, device_id_type=MESH,
        ).start()

    def arrived(dst, recv):
        pltpu.make_async_remote_copy(
            src_ref=dst, dst_ref=dst, send_sem=send_sem.at[0], recv_sem=recv,
            device_id=c_peer, device_id_type=MESH,
        ).wait_recv()

    def finish_sends():
        shape_of = {"f": RY, "s": act.at[0], "d": decw_o, "g": gate.at[0], "h": act.at[0, group[0]], "i": lgp_s.at[0, 0], "e": P.at[0, 0, :, 0]}

        def wait(kind, sem, n):
            ref = RZ.at[0, 0, :n] if kind == "q" else shape_of[kind]
            pltpu.make_async_remote_copy(
                src_ref=ref, dst_ref=ref, send_sem=send_sem.at[sem],
                recv_sem=small_recv.at[0], device_id=c_peer, device_id_type=MESH,
            ).wait_send()

        for who in ("all",) + tuple(flags):
            items = [(kind, sem, n) for (kind, w), sem, n in batches if w == who]

            def go():
                for item in items:
                    wait(*item)
            if who == "all":
                go()
            elif items:
                pl.when(flags[who])(go)

    def group_of(k):
        return t if k == 0 else ot

    class Gather:
        def __init__(self, full, recv, core_recv, swaps):
            self.full, self.recv, self.core_recv, self.swaps = full, recv, core_recv, swaps

        def ref(self, p, zz, xx):
            cc, tt = p
            sem = self.recv.at[((cc * 2 + tt) * NZ + zz) * NX + xx]
            return self.full.at[cc, tt, zz, xx, :, qc], sem

        def give(self, p, zz, xx, peer, who="all"):
            ref, sem = self.ref(p, zz, xx)
            push("q", ref, ref, sem, peer, who)

        def own(self, p):
            self.give(p, z, x, x_peer)
            self.give(p, z, x, pair)
            pl.when(inside)(lambda: self.give(p, z, x, inner, "inside"))

        def along_z(self, p, i):
            zz = sources[i]
            to = inner if i == 0 else pair
            arrived(*self.ref(p, zz, x))
            pl.when(inside)(lambda: self.give(p, zz, x, to, "inside"))
            if i > 0 or p[0] not in self.swaps:
                self.give(p, zz, x, x_peer)

        def across(self, p):
            arrived(*self.ref(p, z, ox))
            self.give(p, z, ox, pair)

        def to_core(self, p, xx, slot):
            cc, tt = p
            ref = self.full.at[cc, tt, :, xx, :, qc]
            push("e", ref, ref, self.core_recv.at[(cc * 2 + tt) * 2 + slot], c_peer)

        def line(self, p):
            self.to_core(p, x, 0)

        def cross(self, p):
            for zz in sources if p[0] in self.swaps else (z,) + sources:
                arrived(*self.ref(p, zz, ox))
            self.to_core(p, ox, 1)

        def settle(self, p, parts=(0, 1)):
            cc, tt = p
            for slot in parts:
                arrived(
                    self.full.at[cc, tt, :, ox if slot else x, :, qo],
                    self.core_recv.at[(cc * 2 + tt) * 2 + slot],
                )

    toks = Gather(X, tok_recv, tokc_recv, ())
    decs = Gather(D, dec_recv, decc_recv, ())

    def tok_own(p):
        cc, k = p
        tt = group_of(k)
        own_sem = own_recv.at[cc * 2 + k]

        @pl.when(c == cc)
        def _():
            src = tok_hbm.at[:, sent_q] if k == 0 else YQ
            if k == 1:
                arrived(YQ, y_recv.at[1])
            push("q", src, X.at[cc, tt, z, x, :, qo], own_sem, c_peer, f"c{cc}")
            if k == 0:
                local[0].wait()
            else:
                arrived(X.at[cc, tt, z, x, :, qc], y_recv.at[0])

        @pl.when(c != cc)
        def _():
            arrived(X.at[cc, tt, z, x, :, qc], own_sem)

        toks.own((cc, tt))

    part = [pl.ds(cc * chunk_rows, chunk_rows) for cc in range(2)]
    group_rows = chunk_rows // 2
    group = [slice(tt * group_rows, (tt + 1) * group_rows) for tt in range(2)]
    tile = 1024

    def encode(p):
        cc, tt = p
        toks.settle(p)
        rows_p = group[tt]
        pre[cc, rows_p, :] = jnp.dot(
            X[cc, tt, :, :, :, :tile].reshape(group_rows, tile), encw[:tile, :],
            preferred_element_type=F32,
        )

        @pl.loop(1, half // tile)
        def _(k):
            cols = pl.ds(pl.multiple_of(k * tile, tile), tile)
            pre[cc, rows_p, :] += jnp.dot(
                X[cc, tt, :, :, :, cols].reshape(group_rows, tile), encw[cols, :],
                preferred_element_type=F32,
            )
        pre_s[cc, rows_p, :] = pre[cc, rows_p, :].astype(BF16)
        swap(pre_s, pre_o, p, 0, y_peer)

    def encode_chunk(cc):
        for tt in range(2):
            toks.settle((cc, tt))
        pre[cc] = jnp.dot(
            X[cc, :, :, :, :, :tile].reshape(chunk_rows, tile), encw[:tile, :],
            preferred_element_type=F32,
        )

        @pl.loop(1, half // tile)
        def _(k):
            cols = pl.ds(pl.multiple_of(k * tile, tile), tile)
            pre[cc] += jnp.dot(
                X[cc, :, :, :, :, cols].reshape(chunk_rows, tile), encw[cols, :],
                preferred_element_type=F32,
            )
        pre_s[cc] = pre[cc].astype(BF16)
        for tt in range(2):
            swap(pre_s, pre_o, (cc, tt), 0, y_peer)

    def swap(src, dst, p, slot, peer):
        cc, tt = p
        push(
            "h", src.at[cc, group[tt]], dst.at[cc, group[tt]],
            small_recv.at[slot + cc * 2 + tt], peer,
        )

    def swapped(dst, p, slot):
        cc, tt = p
        arrived(dst.at[cc, group[tt]], small_recv.at[slot + cc * 2 + tt])

    tile_t = 512

    def transpose_tokens(cc, k):
        cols = slice(k * tile_t, (k + 1) * tile_t)
        XT[cols, part[cc]] = X[cc, :, :, :, :, cols].reshape(chunk_rows, tile_t).T

    seg_rows = locs * rows // block_count

    def segments(tt):
        for b in range(block_count):
            at = (tt * block_count + b) * seg_rows
            yield slice(at, at + seg_rows), gate[tt, b][:1, :]

    def activate(p):
        cc, tt = p
        swapped(pre_o, p, 0)
        for seg, g in segments(tt):
            v = pre[cc, seg, :] + pre_o[cc, seg, :].astype(F32) + encb[...]
            pre[cc, seg, :] = v
            act[cc, seg, :] = (v * jax.nn.sigmoid(v) * g).astype(BF16)
        swap(act, act_o, p, 4, c_peer)

    def slopes(cc):
        act_t[:, part[cc]] = act[cc].T
        for tt in range(2):
            for seg, g in segments(tt):
                v = pre[cc, seg, :]
                sigma = jax.nn.sigmoid(v)
                pre[cc, seg, :] = sigma * (1.0 + v * (1.0 - sigma)) * g

    tile_d = 512

    def decode(p):
        cc, tt = p
        swapped(act_o, p, 4)

        @pl.loop(0, quarter // tile_d)
        def _(k):
            cols = pl.ds(pl.multiple_of(k * tile_d, tile_d), tile_d)
            own_cols = pl.ds(pl.multiple_of(c * quarter + k * tile_d, tile_d), tile_d)
            term = jnp.dot(act[cc, group[tt], :], decw[:, own_cols], preferred_element_type=F32)
            term = term + jnp.dot(
                act_o[cc, group[tt], :], decw_o[:, cols], preferred_element_type=F32
            )
            P[cc, tt, :, :, :, cols] = term.astype(BF16).reshape(NZ, NX, rows, tile_d)
        sum_x(p)

    def add(dst, *terms):
        total = dst[...].astype(F32)
        for other in terms:
            total = total + other[...].astype(F32)
        dst[...] = total.astype(BF16)

    pair_sums = ((0, 1),)

    def sum_x(p):
        cc, tt = p
        at = (cc * 2 + tt) * NZ
        if p in pair_sums:
            push("q", P.at[cc, tt, pair_z, ox], RP.at[cc, tt], rp_recv.at[cc * 2 + tt], pair)
            push("q", P.at[cc, tt, pair_z, x], RZ.at[cc, tt, z], rz_recv.at[at + z], pair)
        for zz in sources[1:] if p in pair_sums else ring + [z]:
            push("q", P.at[cc, tt, zz, ox], RX.at[cc, tt, zz], rx_recv.at[at + zz], x_peer)

    def sum_pair(p):
        cc, tt = p
        mid = P.at[cc, tt, z, ox]
        arrived(RP.at[cc, tt], rp_recv.at[cc * 2 + tt])
        add(mid, RP.at[cc, tt])
        push("q", mid, RX.at[cc, tt, z], rx_recv.at[(cc * 2 + tt) * NZ + z], x_peer)

    def sum_z(p, i):
        cc, tt = p
        at = (cc * 2 + tt) * NZ
        zz = sources[1 + i] if p in pair_sums else ring[i]
        mid = P.at[cc, tt, zz, x]
        arrived(RX.at[cc, tt, zz], rx_recv.at[at + zz])
        add(mid, RX.at[cc, tt, zz])
        push("q", mid, RZ.at[cc, tt, z], rz_recv.at[at + z], (t, place(zz, x)))

    def sum_own(p):
        cc, tt = p
        arrived(RX.at[cc, tt, z], rx_recv.at[(cc * 2 + tt) * NZ + z])
        for zz in sources:
            arrived(RZ.at[cc, tt, zz], rz_recv.at[(cc * 2 + tt) * NZ + zz])
        total = P[cc, tt, z, x].astype(F32) + RX[cc, tt, z].astype(F32)
        for zz in sources:
            total = total + RZ[cc, tt, zz].astype(F32)
        D[cc, tt, z, x, :, qc] = (total + decb[...]).astype(BF16)
        decs.own(p)

    def latent(p):
        cc, tt = p
        decs.settle(p)
        sub = group[tt]
        lg[cc, sub, :] = jnp.zeros((group_rows, latents), F32)

        @pl.loop(0, half // tile)
        def _(k):
            cols = pl.ds(pl.multiple_of(k * tile, tile), tile)
            cot = D[cc, tt, :, :, :, cols].astype(F32) - X[cc, tt, :, :, :, cols].astype(F32)
            cot = (cot * cot_scale).astype(BF16)
            C[cc, tt, :, :, :, cols] = cot
            lg[cc, sub, :] += lax.dot_general(
                cot.reshape(group_rows, tile), decw[:, cols],
                (((1,), (1,)), ((), ())), preferred_element_type=F32,
            )
        lg_s[cc, sub, :] = lg[cc, sub, :].astype(BF16)
        swap(lg_s, lg_o, p, 8, y_peer)

    def latent_chunk(cc):
        for tt in range(2):
            decs.settle((cc, tt))
        lg[cc] = jnp.zeros((chunk_rows, latents), F32)

        @pl.loop(0, half // tile)
        def _(k):
            cols = pl.ds(pl.multiple_of(k * tile, tile), tile)
            cot = D[cc, :, :, :, :, cols].astype(F32) - X[cc, :, :, :, :, cols].astype(F32)
            cot = (cot * cot_scale).astype(BF16)
            C[cc, :, :, :, :, cols] = cot
            lg[cc] += lax.dot_general(
                cot.reshape(chunk_rows, tile), decw[:, cols],
                (((1,), (1,)), ((), ())), preferred_element_type=F32,
            )
        lg_s[cc] = lg[cc].astype(BF16)
        for tt in range(2):
            swap(lg_s, lg_o, (cc, tt), 8, y_peer)

    def latent_part(p, slot):
        cc, tt = p
        decs.settle(p, (slot,))
        xx = ox if slot else x
        part_rows = group_rows // NX
        lgp[tt, xx] = jnp.zeros((part_rows, latents), F32)

        @pl.loop(0, half // tile)
        def _(k):
            cols = pl.ds(pl.multiple_of(k * tile, tile), tile)
            cot = D[cc, tt, :, xx, :, cols].astype(F32) - X[cc, tt, :, xx, :, cols].astype(F32)
            cot = (cot * cot_scale).astype(BF16)
            C[cc, tt, :, xx, :, cols] = cot
            lgp[tt, xx] += lax.dot_general(
                cot.reshape(part_rows, tile), decw[:, cols],
                (((1,), (1,)), ((), ())), preferred_element_type=F32,
            )
        lgp_s[tt, xx] = lgp[tt, xx].astype(BF16)
        push(
            "i", lgp_s.at[tt, xx], lgp_o.at[tt, xx], small_recv.at[14 + tt * 2 + slot], y_peer
        )

    def pre_grad_parts(p):
        cc, tt = p
        for slot in range(2):
            arrived(lgp_o.at[tt, ox if slot else x], small_recv.at[14 + tt * 2 + slot])
        for zz in range(NZ):
            for xx in range(NX):
                at = tt * group_rows + (zz * NX + xx) * rows
                row = slice(zz * rows, (zz + 1) * rows)
                pg[cc * chunk_rows + at : cc * chunk_rows + at + rows, :] = (
                    (lgp[tt, xx, row, :] + lgp_o[tt, xx, row, :].astype(F32))
                    * pre[cc, at : at + rows, :]
                ).astype(BF16)

    def send_recon():
        push("f", D.at[c, ot, z, x], RY, y_recv.at[2], y_peer)

    def pre_grad(p):
        cc, tt = p
        sub = group[tt]
        swapped(lg_o, p, 8)
        at = cc * chunk_rows + tt * group_rows
        pg[at : at + group_rows, :] = (
            (lg[cc, sub, :] + lg_o[cc, sub, :].astype(F32)) * pre[cc, sub, :]
        ).astype(BF16)

    push("q", tok_hbm.at[:, y_own_q], X.at[c, t, z, x, :, qc], y_recv.at[0], y_peer)
    push("q", tok_hbm.at[:, y_sent_q], YQ, y_recv.at[1], y_peer)
    p00, p01, p10, p11 = (0, 0), (0, 1), (1, 0), (1, 1)
    tok_own((0, 0))
    tok_own((1, 0))
    local[5].wait()
    for b in range(block_count):
        hit = blocks_ref[b, 0] == l
        for slot in range(1, blocks_ref.shape[1]):
            hit = jnp.logical_or(hit, blocks_ref[b, slot] == l)
        gate[t, b] = jnp.broadcast_to(jnp.where(hit, 1.0, 0.0).astype(F32), gate.shape[2:])
    push("g", gate.at[t], gate.at[t], small_recv.at[12], y_peer)
    toks.along_z((0, t), 0)
    toks.along_z((1, t), 0)
    tok_own((0, 1))
    tok_own((1, 1))
    toks.along_z((0, ot), 0)
    toks.along_z((1, ot), 0)
    push("d", decw_hbm.at[:, sent_q], decw_o, small_recv.at[13], c_peer)
    toks.along_z(p00, 1)
    toks.along_z(p01, 1)
    toks.along_z(p00, 2)
    toks.line(p00)
    toks.along_z(p01, 2)
    toks.line(p01)
    toks.cross(p00)
    local[1].wait()
    toks.along_z(p10, 1)
    toks.along_z(p10, 2)
    toks.cross(p01)
    encode_chunk(0)
    toks.along_z(p11, 1)
    toks.along_z(p11, 2)
    toks.line(p11)
    toks.line(p10)
    local[3].wait()
    arrived(gate.at[ot], small_recv.at[12])
    activate(p00)
    activate(p01)
    local[2].wait()
    arrived(decw_o, small_recv.at[13])
    decode(p00)
    transpose_tokens(0, 1)
    decode(p01)
    transpose_tokens(0, 2)
    toks.cross(p10)
    encode(p10)
    sum_z(p00, 0)
    toks.cross(p11)
    encode(p11)
    transpose_tokens(0, 3)
    local[4].wait()
    transpose_tokens(0, 7)
    transpose_tokens(0, 4)
    sum_z(p00, 1)
    transpose_tokens(0, 5)
    transpose_tokens(0, 0)
    activate(p10)
    sum_z(p00, 2)
    transpose_tokens(0, 6)
    decode(p10)
    activate(p11)
    sum_z(p01, 0)
    sum_pair(p01)
    decode(p11)
    slopes(0)
    transpose_tokens(1, 6)
    sum_z(p01, 1)
    transpose_tokens(1, 0)
    transpose_tokens(1, 1)
    sum_own(p00)
    transpose_tokens(1, 2)
    sum_z(p10, 0)
    transpose_tokens(1, 3)
    decs.along_z(p00, 0)
    sum_z(p10, 1)
    transpose_tokens(1, 4)
    sum_own(p01)
    sum_z(p10, 2)
    transpose_tokens(1, 5)
    decs.along_z(p00, 1)
    decs.along_z(p01, 0)
    sum_z(p11, 0)
    transpose_tokens(1, 7)
    decs.along_z(p00, 2)
    decs.line(p00)
    sum_z(p11, 1)
    sum_own(p10)
    decs.along_z(p01, 1)
    sum_z(p11, 2)
    decs.along_z(p01, 2)
    decs.line(p01)
    decs.along_z(p10, 0)
    sum_own(p11)
    decs.along_z(p10, 1)
    slopes(1)
    decs.cross(p00)
    decs.along_z(p10, 2)
    decs.line(p10)
    decs.along_z(p11, 0)
    latent_part(p10, 0)
    decs.cross(p01)
    latent_chunk(0)
    decs.along_z(p11, 1)
    decs.along_z(p11, 2)
    decs.line(p11)
    latent_part(p11, 0)
    send_recon()
    pre_grad(p00)
    pre_grad(p01)
    decs.cross(p10)
    latent_part(p10, 1)
    decs.cross(p11)
    latent_part(p11, 1)
    tile_o = 512

    @pl.loop(0, half // tile_o)
    def _(k):
        cols = pl.ds(pl.multiple_of(k * tile_o, tile_o), tile_o)
        dg[:, cols] = jnp.dot(
            act_t[...], C[:, :, :, :, :, cols].reshape(2 * chunk_rows, tile_o),
            preferred_element_type=F32,
        )
    recon_ref[:, mine] = D[c, t, z, x]
    pre_grad_parts(p10)
    finish_sends()
    pre_grad_parts(p11)
    arrived(RY, y_recv.at[2])
    recon_ref[:, theirs] = RY[...]


def grads_kernel(recon_in, xt, pg, dg, recon_out, encg_out, decg_out, eg, sems):
    copies = [
        pltpu.make_async_copy(dg, decg_out, sems.at[0]),
        pltpu.make_async_copy(recon_in, recon_out, sems.at[1]),
    ]
    for copy in copies:
        copy.start()
    tile = 512
    for k in range(xt.shape[0] // tile):
        cols = slice(k * tile, (k + 1) * tile)
        eg[cols, :] = jnp.dot(xt[cols, :], pg[...], preferred_element_type=F32)
        copies.append(
            pltpu.make_async_copy(eg.at[cols], encg_out.at[cols], sems.at[2 + k])
        )
        copies[-1].start()
    for copy in copies:
        copy.wait()


def fused_shards(tokens, enc_weight, enc_bias, dec_weight, dec_bias, active_blocks):
    rows, width = tokens.shape
    lat_count = lax.axis_size("lat")
    tok_count = lax.axis_size("tok")
    group_rows = rows * lat_count
    latents = enc_weight.shape[1]
    half = width // tok_count
    quarter = half // NC
    locs = lat_count // NC
    chunk_rows = 2 * locs * rows
    blocks = active_blocks.shape[0]
    cot_scale = 1.0 / math.sqrt(group_rows * tok_count)
    hbm = pl.BlockSpec(memory_space=pltpu.HBM)
    vmem = pl.BlockSpec(memory_space=pltpu.VMEM)
    dma = pltpu.SemaphoreType.DMA
    pieces = pltpu.VMEM((2, 2, NZ, NX, rows, half), BF16)
    small = pltpu.VMEM((2, chunk_rows, latents), BF16)
    small_f = pltpu.VMEM((2, chunk_rows, latents), F32)

    slots = pltpu.VMEM((2, 2, NZ, rows, quarter), BF16)
    inputs = [
        pltpu.with_memory_space_constraint(a, pltpu.HBM)
        for a in (
            tokens, enc_weight, enc_bias[None, :], dec_weight, dec_bias[None, :], active_blocks
        )
    ]
    recon, xt, pg, dg = pl.pallas_call(
        functools.partial(fused_kernel, cot_scale),
        out_shape=(
            jax.ShapeDtypeStruct((rows, width), BF16),
            jax.ShapeDtypeStruct((half, 2 * chunk_rows), BF16),
            jax.ShapeDtypeStruct((2 * chunk_rows, latents), BF16),
            jax.ShapeDtypeStruct((latents, half), F32),
        ),
        in_specs=[hbm] * 6,
        out_specs=(vmem,) * 4,
        scratch_shapes=[
            pltpu.VMEM((half, latents), BF16),
            pltpu.VMEM((latents, half), BF16),
            pltpu.VMEM((latents, quarter), BF16),
            pltpu.VMEM((1, latents), F32),
            pltpu.VMEM((1, quarter), F32),
            pltpu.VMEM((rows, quarter), BF16),
            pltpu.VMEM((rows, half), BF16),
            pieces,
            pieces,
            pieces,
            pltpu.VMEM((2, 2, NZ, NX, rows, quarter), BF16),
            slots, slots,
            pltpu.VMEM((2, 2, rows, quarter), BF16),
            small_f, small, small, small, small,
            pltpu.VMEM((latents, 2 * chunk_rows), BF16),
            small_f, small, small,
            pltpu.VMEM((2, NX, chunk_rows // 4, latents), F32),
            pltpu.VMEM((2, NX, chunk_rows // 4, latents), BF16),
            pltpu.VMEM((2, NX, chunk_rows // 4, latents), BF16),
            pltpu.VMEM((tok_count, blocks, 8, latents), F32),
            pltpu.SMEM(active_blocks.shape, jnp.int32),
            dma((6,)), dma((80,)), dma((3,)), dma((4,)),
            dma((32,)), dma((8,)), dma((32,)), dma((8,)),
            dma((16,)), dma((16,)), dma((4,)), dma((18,)),
        ],
        compiler_params=pltpu.CompilerParams(
            collective_id=0, has_side_effects=True, vmem_limit_bytes=40 * 1024 * 1024
        ),
        name="fused_step",
    )(*inputs)
    return pl.pallas_call(
        grads_kernel,
        out_shape=(
            jax.ShapeDtypeStruct((rows, width), BF16),
            jax.ShapeDtypeStruct((half, latents), F32),
            jax.ShapeDtypeStruct((latents, half), F32),
        ),
        in_specs=[vmem] * 4,
        out_specs=(hbm,) * 3,
        scratch_shapes=[pltpu.VMEM((half, latents), F32), dma((2 + half // 512,))],
        compiler_params=pltpu.CompilerParams(vmem_limit_bytes=16 * 1024 * 1024),
        name="weight_grads",
    )(recon, xt, pg, dg)


def shards(tokens, enc_weight, enc_bias, dec_weight, dec_bias, active_blocks):
    tok_dev = tokens.shape[0]
    lat_count = lax.axis_size("lat")
    tok_count = lax.axis_size("tok")
    group_rows = tok_dev * lat_count
    latent_width = enc_weight.shape[1]
    block_count = active_blocks.shape[0]
    block_rows = group_rows // block_count
    blocks_here = latent_width // LB
    owner_index = lax.axis_index("lat")
    cot_scale = 1.0 / math.sqrt(group_rows * tok_count)
    block_ids = owner_index * blocks_here + jnp.arange(blocks_here, dtype=jnp.int32)
    block_hits = jnp.any(active_blocks[:, :, None] == block_ids[None, None, :], axis=1).astype(
        jnp.float32
    )
    latent_gate = jnp.repeat(block_hits, LB, axis=1)[:, None, :]
    bias_row = enc_bias[None, None, :]
    gathered = lax.all_gather(tokens, "lat", axis=0, tiled=True)
    pre_act = (
        jnp.dot(gathered, enc_weight, preferred_element_type=jnp.float32).reshape(
            block_count, block_rows, latent_width
        )
        + bias_row
    )
    activations = (
        (jax.nn.silu(pre_act) * latent_gate).astype(jnp.bfloat16).reshape(group_rows, latent_width)
    )
    bias_dec = dec_bias[None, :]
    partial_sum = jnp.dot(activations, dec_weight, preferred_element_type=jnp.float32)
    decoded_all = lax.psum(partial_sum.astype(jnp.bfloat16), "lat").astype(jnp.float32) + bias_dec
    cot_all = ((decoded_all - gathered.astype(jnp.float32)) * cot_scale).astype(jnp.bfloat16)
    decoded = lax.dynamic_slice_in_dim(decoded_all, owner_index * tok_dev, tok_dev, 0)
    dec_local = contract_rows(activations, cot_all)
    latent_grad = lax.dot_general(
        cot_all, dec_weight, (((1,), (1,)), ((), ())), preferred_element_type=jnp.float32
    )
    sigma = jax.nn.sigmoid(pre_act)
    slope = sigma * (1.0 + pre_act * (1.0 - sigma))
    pre_grad = (
        (latent_grad.reshape(block_count, block_rows, latent_width) * slope * latent_gate)
        .astype(jnp.bfloat16)
        .reshape(group_rows, latent_width)
    )
    enc_local = contract_rows(gathered, pre_grad)
    enc_grad, dec_grad = (
        lax.psum_scatter(
            enc_local.astype(jnp.bfloat16), "tok", scatter_dimension=0, tiled=True
        ).astype(jnp.float32),
        lax.psum_scatter(
            dec_local.astype(jnp.bfloat16), "tok", scatter_dimension=1, tiled=True
        ).astype(jnp.float32),
    )
    return (decoded.astype(jnp.bfloat16), enc_grad, dec_grad)


def solution(mesh):
    placed = (
        P(("tok", "lat"), None),
        P(None, "lat"),
        P("lat"),
        P("lat", None),
        P(),
        P("tok", None),
    )
    fits = mesh.shape["tok"] == 2 and mesh.shape["lat"] == NZ * NX * NC
    return jax.shard_map(
        fused_shards if fits else shards,
        mesh=mesh,
        in_specs=placed,
        out_specs=(P(("tok", "lat"), None), P("tok", "lat"), P("lat", "tok")),
        check_vma=False,
    )
```

```python
import functools
import math

import jax
import jax.numpy as jnp
from jax import lax
from jax.experimental import pallas as pl
from jax.experimental.pallas import tpu as pltpu
from jax.sharding import PartitionSpec as P

LB = 256
MESH = pl.DeviceIdType.MESH
NZ, NX, NC = 4, 2, 2
Z_ORDER = (2, 1, 3)
BF16 = jnp.bfloat16
F32 = jnp.float32


def contract_rows(left_rows, right_rows):
    return lax.dot_general(
        left_rows, right_rows, (((0,), (0,)), ((), ())), preferred_element_type=jnp.float32
    )


def fused_kernel(
    cot_scale,
    tok_hbm, encw_hbm, encb_hbm, decw_hbm, decb_hbm, blocks_hbm,
    recon_ref, XT, pg, dg,
    encw, decw, decw_o, encb, decb, YQ, RY, X, D, C, P, RX, RZ, RP,
    pre, pre_s, pre_o, act, act_o, act_t, lg, lg_s, lg_o, lgp, lgp_s, lgp_o, gate, blocks_ref,
    local_sem, send_sem, y_recv, own_recv, tok_recv, tokc_recv, dec_recv, decc_recv,
    rx_recv, rz_recv, rp_recv, small_recv,
):
    t = lax.axis_index("tok")
    l = lax.axis_index("lat")
    z, x, c = l // (NX * NC), (l // NC) % NX, l % NC
    rows, width = tok_hbm.shape
    half = width // 2
    quarter = half // 2
    locs = NZ * NX
    chunk_rows = 2 * locs * rows
    latents = encw.shape[1]

    ox, ot = 1 - x, 1 - t
    pair_z = z + 1 - 2 * lax.rem(z, 2)
    near = z // 2
    sources = (pair_z, 2 - near, 3 - 3 * near)
    ring = [lax.rem(z + dz, NZ) for dz in Z_ORDER]
    inside = jnp.logical_and(z >= 1, z <= 2)

    def place(zz, xx):
        return (zz * NX + xx) * NC + c

    pair = (t, place(pair_z, x))
    inner = (t, place(3 - z, x))
    x_peer = (t, place(z, ox))
    c_peer = (t, (z * NX + x) * NC + 1 - c)
    y_peer = (ot, l)

    mine = pl.ds(pl.multiple_of(t * half, half), half)
    theirs = pl.ds(pl.multiple_of(ot * half, half), half)
    qc = pl.ds(pl.multiple_of(c * quarter, quarter), quarter)
    qo = pl.ds(pl.multiple_of((1 - c) * quarter, quarter), quarter)
    sent_q = pl.ds(pl.multiple_of(t * half + (1 - c) * quarter, quarter), quarter)

    own_q = pl.ds(pl.multiple_of(t * half + c * quarter, quarter), quarter)
    y_own_q = pl.ds(pl.multiple_of(ot * half + c * quarter, quarter), quarter)
    y_sent_q = pl.ds(pl.multiple_of(ot * half + (1 - c) * quarter, quarter), quarter)

    local = [
        pltpu.make_async_copy(tok_hbm.at[:, own_q], X.at[c, t, z, x, :, qc], local_sem.at[0]),
        pltpu.make_async_copy(encw_hbm.at[mine], encw, local_sem.at[1]),
        pltpu.make_async_copy(decw_hbm.at[:, mine], decw, local_sem.at[2]),
        pltpu.make_async_copy(encb_hbm, encb, local_sem.at[3]),
        pltpu.make_async_copy(decb_hbm.at[:, own_q], decb, local_sem.at[4]),
        pltpu.make_async_copy(blocks_hbm, blocks_ref, local_sem.at[5]),
    ]
    for copy in local:
        copy.start()

    block_count = blocks_ref.shape[0]
    barrier = pltpu.get_barrier_semaphore()
    for peer in (pair, x_peer, c_peer, y_peer):
        pl.semaphore_signal(barrier, inc=1, device_id=peer, device_id_type=MESH)

    @pl.when(inside)
    def _():
        pl.semaphore_signal(barrier, inc=1, device_id=inner, device_id_type=MESH)
        pl.semaphore_wait(barrier, 5)

    @pl.when(jnp.logical_not(inside))
    def _():
        pl.semaphore_wait(barrier, 4)

    flags = {"inside": inside, "c0": c == 0, "c1": c == 1}
    sems = [0]
    batches = []

    def push(kind, src, dst, recv, peer, who="all"):
        for batch in batches:
            if batch[0] == (kind, who) and kind == "q" and batch[2] < NZ:
                break
        else:
            batch = [(kind, who), sems[0], 0]
            batches.append(batch)
            sems[0] += 1
        batch[2] += 1
        pltpu.make_async_remote_copy(
            src_ref=src, dst_ref=dst, send_sem=send_sem.at[batch[1]], recv_sem=recv,
            device_id=peer, device_id_type=MESH,
        ).start()

    def arrived(dst, recv):
        pltpu.make_async_remote_copy(
            src_ref=dst, dst_ref=dst, send_sem=send_sem.at[0], recv_sem=recv,
            device_id=c_peer, device_id_type=MESH,
        ).wait_recv()

    def finish_sends():
        shape_of = {"f": RY, "s": act.at[0], "d": decw_o, "g": gate.at[0], "h": act.at[0, group[0]], "i": lgp_s.at[0, 0], "e": P.at[0, 0, :, 0]}

        def wait(kind, sem, n):
            ref = RZ.at[0, 0, :n] if kind == "q" else shape_of[kind]
            pltpu.make_async_remote_copy(
                src_ref=ref, dst_ref=ref, send_sem=send_sem.at[sem],
                recv_sem=small_recv.at[0], device_id=c_peer, device_id_type=MESH,
            ).wait_send()

        for who in ("all",) + tuple(flags):
            items = [(kind, sem, n) for (kind, w), sem, n in batches if w == who]

            def go():
                for item in items:
                    wait(*item)
            if who == "all":
                go()
            elif items:
                pl.when(flags[who])(go)

    def group_of(k):
        return t if k == 0 else ot

    class Gather:
        def __init__(self, full, recv, core_recv, swaps):
            self.full, self.recv, self.core_recv, self.swaps = full, recv, core_recv, swaps

        def ref(self, p, zz, xx):
            cc, tt = p
            sem = self.recv.at[((cc * 2 + tt) * NZ + zz) * NX + xx]
            return self.full.at[cc, tt, zz, xx, :, qc], sem

        def give(self, p, zz, xx, peer, who="all"):
            ref, sem = self.ref(p, zz, xx)
            push("q", ref, ref, sem, peer, who)

        def own(self, p):
            self.give(p, z, x, x_peer)
            self.give(p, z, x, pair)
            pl.when(inside)(lambda: self.give(p, z, x, inner, "inside"))

        def along_z(self, p, i):
            zz = sources[i]
            to = inner if i == 0 else pair
            arrived(*self.ref(p, zz, x))
            pl.when(inside)(lambda: self.give(p, zz, x, to, "inside"))
            if i > 0 or p[0] not in self.swaps:
                self.give(p, zz, x, x_peer)

        def across(self, p):
            arrived(*self.ref(p, z, ox))
            self.give(p, z, ox, pair)

        def to_core(self, p, xx, slot):
            cc, tt = p
            ref = self.full.at[cc, tt, :, xx, :, qc]
            push("e", ref, ref, self.core_recv.at[(cc * 2 + tt) * 2 + slot], c_peer)

        def line(self, p):
            self.to_core(p, x, 0)

        def cross(self, p):
            for zz in sources if p[0] in self.swaps else (z,) + sources:
                arrived(*self.ref(p, zz, ox))
            self.to_core(p, ox, 1)

        def settle(self, p, parts=(0, 1)):
            cc, tt = p
            for slot in parts:
                arrived(
                    self.full.at[cc, tt, :, ox if slot else x, :, qo],
                    self.core_recv.at[(cc * 2 + tt) * 2 + slot],
                )

    toks = Gather(X, tok_recv, tokc_recv, ())
    decs = Gather(D, dec_recv, decc_recv, ())

    def tok_own(p):
        cc, k = p
        tt = group_of(k)
        own_sem = own_recv.at[cc * 2 + k]

        @pl.when(c == cc)
        def _():
            src = tok_hbm.at[:, sent_q] if k == 0 else YQ
            if k == 1:
                arrived(YQ, y_recv.at[1])
            push("q", src, X.at[cc, tt, z, x, :, qo], own_sem, c_peer, f"c{cc}")
            if k == 0:
                local[0].wait()
            else:
                arrived(X.at[cc, tt, z, x, :, qc], y_recv.at[0])

        @pl.when(c != cc)
        def _():
            arrived(X.at[cc, tt, z, x, :, qc], own_sem)

        toks.own((cc, tt))

    part = [pl.ds(cc * chunk_rows, chunk_rows) for cc in range(2)]
    group_rows = chunk_rows // 2
    group = [slice(tt * group_rows, (tt + 1) * group_rows) for tt in range(2)]
    tile = 1024

    def encode(p):
        cc, tt = p
        toks.settle(p)
        rows_p = group[tt]
        pre[cc, rows_p, :] = jnp.dot(
            X[cc, tt, :, :, :, :tile].reshape(group_rows, tile), encw[:tile, :],
            preferred_element_type=F32,
        )

        @pl.loop(1, half // tile)
        def _(k):
            cols = pl.ds(pl.multiple_of(k * tile, tile), tile)
            pre[cc, rows_p, :] += jnp.dot(
                X[cc, tt, :, :, :, cols].reshape(group_rows, tile), encw[cols, :],
                preferred_element_type=F32,
            )
        pre_s[cc, rows_p, :] = pre[cc, rows_p, :].astype(BF16)
        swap(pre_s, pre_o, p, 0, y_peer)

    def encode_chunk(cc):
        for tt in range(2):
            toks.settle((cc, tt))
        pre[cc] = jnp.dot(
            X[cc, :, :, :, :, :tile].reshape(chunk_rows, tile), encw[:tile, :],
            preferred_element_type=F32,
        )

        @pl.loop(1, half // tile)
        def _(k):
            cols = pl.ds(pl.multiple_of(k * tile, tile), tile)
            pre[cc] += jnp.dot(
                X[cc, :, :, :, :, cols].reshape(chunk_rows, tile), encw[cols, :],
                preferred_element_type=F32,
            )
        pre_s[cc] = pre[cc].astype(BF16)
        for tt in range(2):
            swap(pre_s, pre_o, (cc, tt), 0, y_peer)

    def swap(src, dst, p, slot, peer):
        cc, tt = p
        push(
            "h", src.at[cc, group[tt]], dst.at[cc, group[tt]],
            small_recv.at[slot + cc * 2 + tt], peer,
        )

    def swapped(dst, p, slot):
        cc, tt = p
        arrived(dst.at[cc, group[tt]], small_recv.at[slot + cc * 2 + tt])

    tile_t = 512

    def transpose_tokens(cc, k):
        cols = slice(k * tile_t, (k + 1) * tile_t)
        XT[cols, part[cc]] = X[cc, :, :, :, :, cols].reshape(chunk_rows, tile_t).T

    seg_rows = locs * rows // block_count

    def segments(tt):
        for b in range(block_count):
            at = (tt * block_count + b) * seg_rows
            yield slice(at, at + seg_rows), gate[tt, b][:1, :]

    def activate(p):
        cc, tt = p
        swapped(pre_o, p, 0)
        for seg, g in segments(tt):
            v = pre[cc, seg, :] + pre_o[cc, seg, :].astype(F32) + encb[...]
            pre[cc, seg, :] = v
            act[cc, seg, :] = (v * jax.nn.sigmoid(v) * g).astype(BF16)
        swap(act, act_o, p, 4, c_peer)

    def slopes(cc):
        act_t[:, part[cc]] = act[cc].T
        for tt in range(2):
            for seg, g in segments(tt):
                v = pre[cc, seg, :]
                sigma = jax.nn.sigmoid(v)
                pre[cc, seg, :] = sigma * (1.0 + v * (1.0 - sigma)) * g

    tile_d = 512

    def decode(p):
        cc, tt = p
        swapped(act_o, p, 4)

        @pl.loop(0, quarter // tile_d)
        def _(k):
            cols = pl.ds(pl.multiple_of(k * tile_d, tile_d), tile_d)
            own_cols = pl.ds(pl.multiple_of(c * quarter + k * tile_d, tile_d), tile_d)
            term = jnp.dot(act[cc, group[tt], :], decw[:, own_cols], preferred_element_type=F32)
            term = term + jnp.dot(
                act_o[cc, group[tt], :], decw_o[:, cols], preferred_element_type=F32
            )
            P[cc, tt, :, :, :, cols] = term.astype(BF16).reshape(NZ, NX, rows, tile_d)
        sum_x(p)

    def add(dst, *terms):
        total = dst[...].astype(F32)
        for other in terms:
            total = total + other[...].astype(F32)
        dst[...] = total.astype(BF16)

    pair_sums = ((0, 1),)

    def sum_x(p):
        cc, tt = p
        at = (cc * 2 + tt) * NZ
        if p in pair_sums:
            push("q", P.at[cc, tt, pair_z, ox], RP.at[cc, tt], rp_recv.at[cc * 2 + tt], pair)
            push("q", P.at[cc, tt, pair_z, x], RZ.at[cc, tt, z], rz_recv.at[at + z], pair)
        for zz in sources[1:] if p in pair_sums else ring + [z]:
            push("q", P.at[cc, tt, zz, ox], RX.at[cc, tt, zz], rx_recv.at[at + zz], x_peer)

    def sum_pair(p):
        cc, tt = p
        mid = P.at[cc, tt, z, ox]
        arrived(RP.at[cc, tt], rp_recv.at[cc * 2 + tt])
        add(mid, RP.at[cc, tt])
        push("q", mid, RX.at[cc, tt, z], rx_recv.at[(cc * 2 + tt) * NZ + z], x_peer)

    def sum_z(p, i):
        cc, tt = p
        at = (cc * 2 + tt) * NZ
        zz = sources[1 + i] if p in pair_sums else ring[i]
        mid = P.at[cc, tt, zz, x]
        arrived(RX.at[cc, tt, zz], rx_recv.at[at + zz])
        add(mid, RX.at[cc, tt, zz])
        push("q", mid, RZ.at[cc, tt, z], rz_recv.at[at + z], (t, place(zz, x)))

    def sum_own(p):
        cc, tt = p
        arrived(RX.at[cc, tt, z], rx_recv.at[(cc * 2 + tt) * NZ + z])
        for zz in sources:
            arrived(RZ.at[cc, tt, zz], rz_recv.at[(cc * 2 + tt) * NZ + zz])
        total = P[cc, tt, z, x].astype(F32) + RX[cc, tt, z].astype(F32)
        for zz in sources:
            total = total + RZ[cc, tt, zz].astype(F32)
        D[cc, tt, z, x, :, qc] = (total + decb[...]).astype(BF16)
        decs.own(p)

    def latent(p):
        cc, tt = p
        decs.settle(p)
        sub = group[tt]
        lg[cc, sub, :] = jnp.zeros((group_rows, latents), F32)

        @pl.loop(0, half // tile)
        def _(k):
            cols = pl.ds(pl.multiple_of(k * tile, tile), tile)
            cot = D[cc, tt, :, :, :, cols].astype(F32) - X[cc, tt, :, :, :, cols].astype(F32)
            cot = (cot * cot_scale).astype(BF16)
            C[cc, tt, :, :, :, cols] = cot
            lg[cc, sub, :] += lax.dot_general(
                cot.reshape(group_rows, tile), decw[:, cols],
                (((1,), (1,)), ((), ())), preferred_element_type=F32,
            )
        lg_s[cc, sub, :] = lg[cc, sub, :].astype(BF16)
        swap(lg_s, lg_o, p, 8, y_peer)

    def latent_chunk(cc):
        for tt in range(2):
            decs.settle((cc, tt))
        lg[cc] = jnp.zeros((chunk_rows, latents), F32)

        @pl.loop(0, half // tile)
        def _(k):
            cols = pl.ds(pl.multiple_of(k * tile, tile), tile)
            cot = D[cc, :, :, :, :, cols].astype(F32) - X[cc, :, :, :, :, cols].astype(F32)
            cot = (cot * cot_scale).astype(BF16)
            C[cc, :, :, :, :, cols] = cot
            lg[cc] += lax.dot_general(
                cot.reshape(chunk_rows, tile), decw[:, cols],
                (((1,), (1,)), ((), ())), preferred_element_type=F32,
            )
        lg_s[cc] = lg[cc].astype(BF16)
        for tt in range(2):
            swap(lg_s, lg_o, (cc, tt), 8, y_peer)

    def latent_part(p, slot):
        cc, tt = p
        decs.settle(p, (slot,))
        xx = ox if slot else x
        part_rows = group_rows // NX
        lgp[tt, xx] = jnp.zeros((part_rows, latents), F32)

        @pl.loop(0, half // tile)
        def _(k):
            cols = pl.ds(pl.multiple_of(k * tile, tile), tile)
            cot = D[cc, tt, :, xx, :, cols].astype(F32) - X[cc, tt, :, xx, :, cols].astype(F32)
            cot = (cot * cot_scale).astype(BF16)
            C[cc, tt, :, xx, :, cols] = cot
            lgp[tt, xx] += lax.dot_general(
                cot.reshape(part_rows, tile), decw[:, cols],
                (((1,), (1,)), ((), ())), preferred_element_type=F32,
            )
        lgp_s[tt, xx] = lgp[tt, xx].astype(BF16)
        push(
            "i", lgp_s.at[tt, xx], lgp_o.at[tt, xx], small_recv.at[14 + tt * 2 + slot], y_peer
        )

    def pre_grad_parts(p):
        cc, tt = p
        for slot in range(2):
            arrived(lgp_o.at[tt, ox if slot else x], small_recv.at[14 + tt * 2 + slot])
        for zz in range(NZ):
            for xx in range(NX):
                at = tt * group_rows + (zz * NX + xx) * rows
                row = slice(zz * rows, (zz + 1) * rows)
                pg[cc * chunk_rows + at : cc * chunk_rows + at + rows, :] = (
                    (lgp[tt, xx, row, :] + lgp_o[tt, xx, row, :].astype(F32))
                    * pre[cc, at : at + rows, :]
                ).astype(BF16)

    def send_recon():
        push("f", D.at[c, ot, z, x], RY, y_recv.at[2], y_peer)

    def pre_grad(p):
        cc, tt = p
        sub = group[tt]
        swapped(lg_o, p, 8)
        at = cc * chunk_rows + tt * group_rows
        pg[at : at + group_rows, :] = (
            (lg[cc, sub, :] + lg_o[cc, sub, :].astype(F32)) * pre[cc, sub, :]
        ).astype(BF16)

    push("q", tok_hbm.at[:, y_own_q], X.at[c, t, z, x, :, qc], y_recv.at[0], y_peer)
    push("q", tok_hbm.at[:, y_sent_q], YQ, y_recv.at[1], y_peer)
    p00, p01, p10, p11 = (0, 0), (0, 1), (1, 0), (1, 1)
    tok_own((0, 0))
    tok_own((1, 0))
    local[5].wait()
    for b in range(block_count):
        hit = blocks_ref[b, 0] == l
        for slot in range(1, blocks_ref.shape[1]):
            hit = jnp.logical_or(hit, blocks_ref[b, slot] == l)
        gate[t, b] = jnp.broadcast_to(jnp.where(hit, 1.0, 0.0).astype(F32), gate.shape[2:])
    push("g", gate.at[t], gate.at[t], small_recv.at[12], y_peer)
    toks.along_z((0, t), 0)
    toks.along_z((1, t), 0)
    tok_own((0, 1))
    tok_own((1, 1))
    toks.along_z((0, ot), 0)
    toks.along_z((1, ot), 0)
    push("d", decw_hbm.at[:, sent_q], decw_o, small_recv.at[13], c_peer)
    toks.along_z(p00, 1)
    toks.along_z(p01, 1)
    toks.along_z(p00, 2)
    toks.line(p00)
    toks.along_z(p01, 2)
    toks.line(p01)
    toks.cross(p00)
    local[1].wait()
    toks.along_z(p10, 1)
    toks.along_z(p10, 2)
    toks.cross(p01)
    encode_chunk(0)
    toks.along_z(p11, 1)
    toks.along_z(p11, 2)
    toks.line(p11)
    toks.line(p10)
    local[3].wait()
    arrived(gate.at[ot], small_recv.at[12])
    activate(p00)
    activate(p01)
    local[2].wait()
    arrived(decw_o, small_recv.at[13])
    decode(p00)
    transpose_tokens(0, 1)
    decode(p01)
    transpose_tokens(0, 2)
    toks.cross(p10)
    encode(p10)
    sum_z(p00, 0)
    toks.cross(p11)
    encode(p11)
    transpose_tokens(0, 3)
    local[4].wait()
    transpose_tokens(0, 7)
    transpose_tokens(0, 4)
    sum_z(p00, 1)
    transpose_tokens(0, 5)
    transpose_tokens(0, 0)
    activate(p10)
    sum_z(p00, 2)
    transpose_tokens(0, 6)
    decode(p10)
    activate(p11)
    sum_z(p01, 0)
    sum_pair(p01)
    decode(p11)
    slopes(0)
    transpose_tokens(1, 6)
    sum_z(p01, 1)
    transpose_tokens(1, 0)
    transpose_tokens(1, 1)
    sum_own(p00)
    transpose_tokens(1, 2)
    sum_z(p10, 0)
    transpose_tokens(1, 3)
    decs.along_z(p00, 0)
    sum_z(p10, 1)
    transpose_tokens(1, 4)
    sum_own(p01)
    sum_z(p10, 2)
    transpose_tokens(1, 5)
    decs.along_z(p00, 1)
    decs.along_z(p01, 0)
    sum_z(p11, 0)
    transpose_tokens(1, 7)
    decs.along_z(p00, 2)
    decs.line(p00)
    sum_z(p11, 1)
    sum_own(p10)
    decs.along_z(p01, 1)
    sum_z(p11, 2)
    decs.along_z(p01, 2)
    decs.line(p01)
    decs.along_z(p10, 0)
    sum_own(p11)
    decs.along_z(p10, 1)
    slopes(1)
    decs.cross(p00)
    decs.along_z(p10, 2)
    decs.line(p10)
    decs.cross(p01)
    latent_chunk(0)
    decs.along_z(p11, 0)
    latent_part(p10, 0)
    decs.along_z(p11, 1)
    decs.along_z(p11, 2)
    decs.line(p11)
    latent_part(p11, 0)
    send_recon()
    pre_grad(p00)
    pre_grad(p01)
    decs.cross(p10)
    latent_part(p10, 1)
    decs.cross(p11)
    latent_part(p11, 1)
    tile_o = 512

    @pl.loop(0, half // tile_o)
    def _(k):
        cols = pl.ds(pl.multiple_of(k * tile_o, tile_o), tile_o)
        dg[:, cols] = jnp.dot(
            act_t[...], C[:, :, :, :, :, cols].reshape(2 * chunk_rows, tile_o),
            preferred_element_type=F32,
        )
    recon_ref[:, mine] = D[c, t, z, x]
    pre_grad_parts(p10)
    finish_sends()
    pre_grad_parts(p11)
    arrived(RY, y_recv.at[2])
    recon_ref[:, theirs] = RY[...]


def grads_kernel(recon_in, xt, pg, dg, recon_out, encg_out, decg_out, eg, sems):
    copies = [
        pltpu.make_async_copy(dg, decg_out, sems.at[0]),
        pltpu.make_async_copy(recon_in, recon_out, sems.at[1]),
    ]
    for copy in copies:
        copy.start()
    tile = 512
    for k in range(xt.shape[0] // tile):
        cols = slice(k * tile, (k + 1) * tile)
        eg[cols, :] = jnp.dot(xt[cols, :], pg[...], preferred_element_type=F32)
        copies.append(
            pltpu.make_async_copy(eg.at[cols], encg_out.at[cols], sems.at[2 + k])
        )
        copies[-1].start()
    for copy in copies:
        copy.wait()


def fused_shards(tokens, enc_weight, enc_bias, dec_weight, dec_bias, active_blocks):
    rows, width = tokens.shape
    lat_count = lax.axis_size("lat")
    tok_count = lax.axis_size("tok")
    group_rows = rows * lat_count
    latents = enc_weight.shape[1]
    half = width // tok_count
    quarter = half // NC
    locs = lat_count // NC
    chunk_rows = 2 * locs * rows
    blocks = active_blocks.shape[0]
    cot_scale = 1.0 / math.sqrt(group_rows * tok_count)
    hbm = pl.BlockSpec(memory_space=pltpu.HBM)
    vmem = pl.BlockSpec(memory_space=pltpu.VMEM)
    dma = pltpu.SemaphoreType.DMA
    pieces = pltpu.VMEM((2, 2, NZ, NX, rows, half), BF16)
    small = pltpu.VMEM((2, chunk_rows, latents), BF16)
    small_f = pltpu.VMEM((2, chunk_rows, latents), F32)

    slots = pltpu.VMEM((2, 2, NZ, rows, quarter), BF16)
    inputs = [
        pltpu.with_memory_space_constraint(a, pltpu.HBM)
        for a in (
            tokens, enc_weight, enc_bias[None, :], dec_weight, dec_bias[None, :], active_blocks
        )
    ]
    recon, xt, pg, dg = pl.pallas_call(
        functools.partial(fused_kernel, cot_scale),
        out_shape=(
            jax.ShapeDtypeStruct((rows, width), BF16),
            jax.ShapeDtypeStruct((half, 2 * chunk_rows), BF16),
            jax.ShapeDtypeStruct((2 * chunk_rows, latents), BF16),
            jax.ShapeDtypeStruct((latents, half), F32),
        ),
        in_specs=[hbm] * 6,
        out_specs=(vmem,) * 4,
        scratch_shapes=[
            pltpu.VMEM((half, latents), BF16),
            pltpu.VMEM((latents, half), BF16),
            pltpu.VMEM((latents, quarter), BF16),
            pltpu.VMEM((1, latents), F32),
            pltpu.VMEM((1, quarter), F32),
            pltpu.VMEM((rows, quarter), BF16),
            pltpu.VMEM((rows, half), BF16),
            pieces,
            pieces,
            pieces,
            pltpu.VMEM((2, 2, NZ, NX, rows, quarter), BF16),
            slots, slots,
            pltpu.VMEM((2, 2, rows, quarter), BF16),
            small_f, small, small, small, small,
            pltpu.VMEM((latents, 2 * chunk_rows), BF16),
            small_f, small, small,
            pltpu.VMEM((2, NX, chunk_rows // 4, latents), F32),
            pltpu.VMEM((2, NX, chunk_rows // 4, latents), BF16),
            pltpu.VMEM((2, NX, chunk_rows // 4, latents), BF16),
            pltpu.VMEM((tok_count, blocks, 8, latents), F32),
            pltpu.SMEM(active_blocks.shape, jnp.int32),
            dma((6,)), dma((61,)), dma((3,)), dma((4,)),
            dma((32,)), dma((8,)), dma((32,)), dma((8,)),
            dma((16,)), dma((16,)), dma((4,)), dma((18,)),
        ],
        compiler_params=pltpu.CompilerParams(
            collective_id=0, has_side_effects=True, vmem_limit_bytes=40 * 1024 * 1024
        ),
        name="fused_step",
    )(*inputs)
    return pl.pallas_call(
        grads_kernel,
        out_shape=(
            jax.ShapeDtypeStruct((rows, width), BF16),
            jax.ShapeDtypeStruct((half, latents), F32),
            jax.ShapeDtypeStruct((latents, half), F32),
        ),
        in_specs=[vmem] * 4,
        out_specs=(hbm,) * 3,
        scratch_shapes=[pltpu.VMEM((half, latents), F32), dma((2 + half // 512,))],
        compiler_params=pltpu.CompilerParams(vmem_limit_bytes=16 * 1024 * 1024),
        name="weight_grads",
    )(recon, xt, pg, dg)


def shards(tokens, enc_weight, enc_bias, dec_weight, dec_bias, active_blocks):
    tok_dev = tokens.shape[0]
    lat_count = lax.axis_size("lat")
    tok_count = lax.axis_size("tok")
    group_rows = tok_dev * lat_count
    latent_width = enc_weight.shape[1]
    block_count = active_blocks.shape[0]
    block_rows = group_rows // block_count
    blocks_here = latent_width // LB
    owner_index = lax.axis_index("lat")
    cot_scale = 1.0 / math.sqrt(group_rows * tok_count)
    block_ids = owner_index * blocks_here + jnp.arange(blocks_here, dtype=jnp.int32)
    block_hits = jnp.any(active_blocks[:, :, None] == block_ids[None, None, :], axis=1).astype(
        jnp.float32
    )
    latent_gate = jnp.repeat(block_hits, LB, axis=1)[:, None, :]
    bias_row = enc_bias[None, None, :]
    gathered = lax.all_gather(tokens, "lat", axis=0, tiled=True)
    pre_act = (
        jnp.dot(gathered, enc_weight, preferred_element_type=jnp.float32).reshape(
            block_count, block_rows, latent_width
        )
        + bias_row
    )
    activations = (
        (jax.nn.silu(pre_act) * latent_gate).astype(jnp.bfloat16).reshape(group_rows, latent_width)
    )
    bias_dec = dec_bias[None, :]
    partial_sum = jnp.dot(activations, dec_weight, preferred_element_type=jnp.float32)
    decoded_all = lax.psum(partial_sum.astype(jnp.bfloat16), "lat").astype(jnp.float32) + bias_dec
    cot_all = ((decoded_all - gathered.astype(jnp.float32)) * cot_scale).astype(jnp.bfloat16)
    decoded = lax.dynamic_slice_in_dim(decoded_all, owner_index * tok_dev, tok_dev, 0)
    dec_local = contract_rows(activations, cot_all)
    latent_grad = lax.dot_general(
        cot_all, dec_weight, (((1,), (1,)), ((), ())), preferred_element_type=jnp.float32
    )
    sigma = jax.nn.sigmoid(pre_act)
    slope = sigma * (1.0 + pre_act * (1.0 - sigma))
    pre_grad = (
        (latent_grad.reshape(block_count, block_rows, latent_width) * slope * latent_gate)
        .astype(jnp.bfloat16)
        .reshape(group_rows, latent_width)
    )
    enc_local = contract_rows(gathered, pre_grad)
    enc_grad, dec_grad = (
        lax.psum_scatter(
            enc_local.astype(jnp.bfloat16), "tok", scatter_dimension=0, tiled=True
        ).astype(jnp.float32),
        lax.psum_scatter(
            dec_local.astype(jnp.bfloat16), "tok", scatter_dimension=1, tiled=True
        ).astype(jnp.float32),
    )
    return (decoded.astype(jnp.bfloat16), enc_grad, dec_grad)


def solution(mesh):
    placed = (
        P(("tok", "lat"), None),
        P(None, "lat"),
        P("lat"),
        P("lat", None),
        P(),
        P("tok", None),
    )
    fits = mesh.shape["tok"] == 2 and mesh.shape["lat"] == NZ * NX * NC
    return jax.shard_map(
        fused_shards if fits else shards,
        mesh=mesh,
        in_specs=placed,
        out_specs=(P(("tok", "lat"), None), P("tok", "lat"), P("lat", "tok")),
        check_vma=False,
    )
```
